32 devices in a mesh: dp: 8 (over z, x), seq: 4 (over y, core).
Axes of the slice: x: 2, y: 2, z: 4, core: 2. Of those that a mesh axis runs over, the one named last changes fastest.
Arguments:
- hidden_states: bfloat16 [32, 512, 768], P('dp', 'seq'), may hold values from -6 to 6
- lengths: int32 [32], P('dp'), may hold values from 20 to 512, as said below
- query_weight: bfloat16 [768, 768], replicated, may hold values from -0.21875 to 0.21875
- query_bias: float32 [768], replicated, may hold values from -3 to 3
- key_weight: bfloat16 [768, 768], replicated, may hold values from -0.21875 to 0.21875
- value_weight: bfloat16 [768, 768], replicated, may hold values from -0.21875 to 0.21875
- value_bias: float32 [768], replicated, may hold values from -3 to 3
- out_weight: bfloat16 [768, 768], replicated, may hold values from -1.75 to 1.75
- out_bias: float32 [768], replicated, may hold values from -2 to 2
- attn_gain: float32 [768], replicated, may hold values from 0.5 to 1.5
- attn_shift: float32 [768], replicated, may hold values from -2 to 2
- inner_weight: bfloat16 [768, 3072], replicated, may hold values from -0.21875 to 0.21875
- inner_bias: float32 [3072], replicated, may hold values from -3 to 3
- outer_weight: bfloat16 [3072, 768], replicated, may hold values from -0.109375 to 0.109375
- outer_bias: float32 [768], replicated, may hold values from -2 to 2
- ffn_gain: float32 [768], replicated, may hold values from 0.5 to 1.5
- ffn_shift: float32 [768], replicated, may hold values from -2 to 2
- cotangent: bfloat16 [32, 512, 768], P('dp', 'seq'), may hold values from -6 to 6
Outputs:
- block_output: bfloat16 [32, 512, 768], P('dp', 'seq')
- input_grad: bfloat16 [32, 512, 768], P('dp', 'seq')
- query_grad: float32 [768, 768], P('dp')
- qbias_grad: float32 [768], P('dp')
- key_grad: float32 [768, 768], P('dp')
- value_grad: float32 [768, 768], P('dp')
- vbias_grad: float32 [768], P('dp')
- out_grad: float32 [768, 768], P('dp')
- obias_grad: float32 [768], P('dp')
- gain1_grad: float32 [768], P('dp')
- shift1_grad: float32 [768], P('dp')
- inner_grad: float32 [768, 3072], P('dp')
- ibias_grad: float32 [3072], P('dp')
- outer_grad: float32 [3072, 768], P('dp')
- fbias_grad: float32 [768], P('dp')
- gain2_grad: float32 [768], P('dp')
- shift2_grad: float32 [768], P('dp')
The draws below stay inside these ranges and needn't reach their ends.
Inputs may be any that keep to these rules, and one draw needn't show every extreme that they name: lengths[p] of the 512 slots of passage p are tokens, the rest padding; every draw has a passage of 512 tokens and one of 20.
All inputs are finite; a program needn't handle non-finite values.
Results may differ from the reference program's by a relative error of at most 0.015.
Values may be sent and summed in bfloat16 or wider, within the bound.
No kernel may reach another device: no remote copies, remote signals or barrier semaphores. Data moves between devices by JAX's collectives and lax.ppermute only.
A program may use at most 192 MiB of HBM per device.

```python
import math
import jax
import jax.numpy as jnp
from jax import lax

D = 768
HEADS = 12
HEAD_DIM = 64
FF = 3072
SEQ = 512
MIN_LEN = 20
PASSAGES = 32


def draw_lengths(key, part):
    subkeys = jax.random.split(jax.random.fold_in(key, 17), 5)
    reach_count = SEQ - MIN_LEN + 1
    draw_one = jax.random.randint(subkeys[0], (PASSAGES,), 0, reach_count)
    draw_two = jax.random.randint(subkeys[1], (PASSAGES,), 0, reach_count)
    draw_three = jax.random.randint(subkeys[2], (PASSAGES,), 0, reach_count)
    shortfall = jnp.minimum(jnp.minimum(draw_one, draw_two), draw_three)
    drawn = SEQ - shortfall
    longest = jax.random.randint(subkeys[3], (), 0, PASSAGES)
    shortest = (longest + 1 + jax.random.randint(subkeys[4], (), 0, PASSAGES - 1)) % PASSAGES
    places = jnp.arange(PASSAGES, dtype=jnp.int32)
    drawn = jnp.where(places == longest, SEQ, drawn)
    drawn = jnp.where(places == shortest, MIN_LEN, drawn)
    return drawn.astype(jnp.int32)


def raised(values, rng, source, target, blocks, factor):
    def block_of(dim):
        return (jnp.arange(values.shape[dim]) // (values.shape[dim] // blocks)).reshape((-1,) + (1,) * (values.ndim - 1 - dim))

    one_side = jax.random.permutation(rng, blocks)[block_of(target)]
    second = (block_of(target) + blocks // 2) % blocks
    return jnp.where((block_of(source) == one_side) | (block_of(source) == second), factor * values, values)


def steps_of(key, dims, pieces, least, largest):
    loudness = 1.0
    for position, parts in pieces:
        draws = jax.random.uniform(jax.random.fold_in(jax.random.fold_in(key, 6), position), (parts,), jnp.float32, least / len(pieces), largest / len(pieces))
        loudness = loudness * jnp.repeat(jnp.exp(draws), dims[position] // parts).reshape((-1,) + (1,) * (len(dims) - 1 - position))
    return loudness


def gaussian(rng, shape, width, reach, pieces=(), kind=jnp.bfloat16):
    entries = width * jax.random.normal(rng, shape, jnp.float32)
    if pieces:
        entries = entries * steps_of(rng, shape, pieces, -0.22, 0.18)
    return jnp.clip(entries, -reach, reach).astype(kind)


def gaussian_with(rng, shape, width, reach, shards, heavy, held_as=jnp.bfloat16):
    array = width * jax.random.normal(rng, shape, jnp.float32)
    if shards:
        array = array * steps_of(rng, shape, shards, -0.22, 0.18)
    return jnp.clip(raised(array, jax.random.fold_in(rng, 3), *heavy), -reach, reach).astype(held_as)


def setup_inputs(seed: int = 0) -> dict:
    key_of = jax.random.split(jax.random.key(seed), 19)
    hidden_states = gaussian(key_of[0], (PASSAGES, SEQ, D), 1.0, 6.0, ((0, 8), (1, 4)))
    lengths = draw_lengths(jax.random.fold_in(key_of[18], 71), 0)
    query_weight = gaussian(key_of[2], (D, D), D ** -0.5, 0.21875)
    query_bias = gaussian(key_of[3], (D,), 0.5, 3.0, (), jnp.float32)
    key_weight = gaussian(key_of[4], (D, D), D ** -0.5, 0.21875)
    value_weight = gaussian(key_of[5], (D, D), D ** -0.5, 0.21875)
    value_bias = gaussian(key_of[6], (D,), 0.5, 3.0, (), jnp.float32)
    out_weight = gaussian(key_of[7], (D, D), (D // 64) ** -0.5, 1.75)
    out_bias = gaussian(key_of[8], (D,), 0.3, 2.0, (), jnp.float32)
    attn_gain = jnp.clip(1.0 + 0.1 * jax.random.normal(key_of[9], (D,), jnp.float32), 0.5, 1.5)
    attn_shift = gaussian(key_of[10], (D,), 0.3, 2.0, (), jnp.float32)
    inner_weight = gaussian(key_of[11], (D, FF), D ** -0.5, 0.21875)
    inner_bias = gaussian(key_of[12], (FF,), 0.5, 3.0, (), jnp.float32)
    outer_weight = gaussian(key_of[13], (FF, D), FF ** -0.5, 0.109375)
    outer_bias = gaussian(key_of[14], (D,), 0.3, 2.0, (), jnp.float32)
    ffn_gain = jnp.clip(1.0 + 0.1 * jax.random.normal(key_of[15], (D,), jnp.float32), 0.5, 1.5)
    ffn_shift = gaussian(key_of[16], (D,), 0.3, 2.0, (), jnp.float32)
    cotangent = gaussian_with(key_of[17], (PASSAGES, SEQ, D), 1.0, 6.0, ((0, 8), (1, 4)), (0, 2, 8, 2.0))
    return {"hidden_states": hidden_states, "lengths": lengths, "query_weight": query_weight, "query_bias": query_bias, "key_weight": key_weight, "value_weight": value_weight, "value_bias": value_bias, "out_weight": out_weight, "out_bias": out_bias, "attn_gain": attn_gain, "attn_shift": attn_shift, "inner_weight": inner_weight, "inner_bias": inner_bias, "outer_weight": outer_weight, "outer_bias": outer_bias, "ffn_gain": ffn_gain, "ffn_shift": ffn_shift, "cotangent": cotangent}


EPSILON = 1e-12
MASKED = -1e+30
HIGHEST = lax.Precision.HIGHEST

@jax.custom_vjp
def low(v):
    return lax.optimization_barrier(v.astype(jnp.bfloat16)).astype(jnp.float32)

@jax.custom_vjp
def low_back(v):
    return v

def low_keep(v):
    return (low(v), None)

def low_pass(kept, grad):
    return (grad,)

def back_keep(v):
    return (v, None)

def back_low(kept, grad):
    return (low(grad),)
low.defvjp(low_keep, low_pass)
low_back.defvjp(back_keep, back_low)

def layer_norm(values, gain, shift):
    center = values - lax.optimization_barrier(jnp.mean(values, -1, keepdims=True))
    spread = lax.optimization_barrier(jnp.mean(center * center, -1, keepdims=True))
    return center * lax.rsqrt(spread + EPSILON) * gain + shift

def matmul(left, right):
    return jnp.einsum('psd,de->pse', left, right, precision=HIGHEST)

def forward(inputs, passage_lengths, query_weight, query_bias, key_weight, value_weight, value_bias, out_weight, out_bias, attn_gain, attn_shift, inner_weight, inner_bias, outer_weight, outer_bias, ffn_gain, ffn_shift):
    passages = inputs.shape[0]
    head_shape = (passages, SEQ, HEADS, HEAD_DIM)
    queries = low_back(low(matmul(inputs, query_weight) + query_bias)).reshape(head_shape)
    key_rows = low_back(low(matmul(inputs, key_weight))).reshape(head_shape)
    value_rows = low_back(low(matmul(inputs, value_weight) + value_bias)).reshape(head_shape)
    scores = jnp.einsum('pqhd,pkhd->phqk', queries, key_rows, precision=HIGHEST) * (1.0 / math.sqrt(HEAD_DIM))
    scores = low_back(scores)
    key_valid = jnp.arange(SEQ, dtype=jnp.int32)[None, :] < passage_lengths[:, None]
    scores = jnp.where(key_valid[:, None, None, :], scores, MASKED)
    row_top = lax.optimization_barrier(jnp.max(scores, -1, keepdims=True))
    shifted_exp = jnp.exp(scores - row_top)
    soft_weights = shifted_exp / lax.optimization_barrier(jnp.sum(shifted_exp, -1, keepdims=True))
    context = jnp.einsum('phqk,pkhd->pqhd', low(soft_weights), value_rows, precision=HIGHEST)
    context = low_back(low(context)).reshape(passages, SEQ, D)
    attention = low_back(matmul(context, out_weight) + out_bias)
    normed = layer_norm(inputs + attention, attn_gain, attn_shift)
    inner = low_back(matmul(low(normed), inner_weight) + inner_bias)
    activated = low(jax.nn.gelu(inner, approximate=False))
    branch = low_back(matmul(activated, outer_weight) + outer_bias)
    return layer_norm(normed + branch, ffn_gain, ffn_shift)

def reference(hidden_states, lengths, query_weight, query_bias, key_weight, value_weight, value_bias, out_weight, out_bias, attn_gain, attn_shift, inner_weight, inner_bias, outer_weight, outer_bias, ffn_gain, ffn_shift, cotangent):
    params = (query_weight.astype(jnp.float32), query_bias.astype(jnp.float32), key_weight.astype(jnp.float32), value_weight.astype(jnp.float32), value_bias.astype(jnp.float32), out_weight.astype(jnp.float32), out_bias.astype(jnp.float32), attn_gain.astype(jnp.float32), attn_shift.astype(jnp.float32), inner_weight.astype(jnp.float32), inner_bias.astype(jnp.float32), outer_weight.astype(jnp.float32), outer_bias.astype(jnp.float32), ffn_gain.astype(jnp.float32), ffn_shift.astype(jnp.float32))
    group_size = math.gcd(PASSAGES, 8)
    group_count = PASSAGES // group_size
    inputs_all = hidden_states.astype(jnp.float32).reshape(group_count, group_size, SEQ, D)
    lengths_all = lengths.reshape(group_count, group_size)
    cotangent_all = cotangent.astype(jnp.float32).reshape(group_count, group_size, SEQ, D)

    def one_group(carry, item):
        group_inputs, group_lengths, group_cotangent = item

        def apply(inputs, *weights):
            return forward(inputs, group_lengths, *weights)
        result, pullback = jax.vjp(apply, group_inputs, *params)
        grads = pullback(group_cotangent)
        updated = tuple((total + piece for total, piece in zip(carry, grads[1:])))
        return (updated, (result.astype(jnp.bfloat16), grads[0].astype(jnp.bfloat16)))
    initial = tuple((jnp.zeros_like(weight) for weight in params))
    sums, (results, input_grads) = lax.scan(one_group, initial, (inputs_all, lengths_all, cotangent_all))
    return (results.reshape(PASSAGES, SEQ, D), input_grads.reshape(PASSAGES, SEQ, D), sums[0], sums[1], sums[2], sums[3], sums[4], sums[5], sums[6], sums[7], sums[8], sums[9], sums[10], sums[11], sums[12], sums[13], sums[14])
```

```python
import math

import jax
import jax.numpy as jnp
from jax import lax
from jax.experimental import pallas as pl
from jax.experimental.pallas import tpu as pltpu
from jax.sharding import PartitionSpec as P

HEAD_DIM = 64
EPSILON = 1e-12
MASKED = -1e30
BF16 = jnp.bfloat16
F32 = jnp.float32
BOTH = ("dp", "seq")


def layer_norm(values, gain, shift):
    center = values - jnp.mean(values, -1, keepdims=True)
    spread = jnp.mean(center * center, -1, keepdims=True)
    return center * lax.rsqrt(spread + EPSILON) * gain + shift


def exact_gelu(values):
    return jax.nn.gelu(values, approximate=False)


def pairs(n_dp, n_seq, partner):
    out = []
    for d in range(n_dp):
        for s in range(n_seq):
            e, t = partner(d, s)
            out.append((d * n_seq + s, e * n_seq + t))
    return out


def swap_seq(n_seq, k):
    return [(s, s ^ k) for s in range(n_seq)]


def pick(blocks, index):
    return lax.dynamic_index_in_dim(blocks, index, 0, keepdims=False)


def exchange(blocks, n_seq):
    return [blocks[0]] + [
        lax.ppermute(blocks[k], "seq", swap_seq(n_seq, k)) for k in range(1, n_seq)
    ]


def bit_orders(n_dp):
    bits = list(range(n_dp.bit_length() - 1))
    return bits, bits[1:] + bits[:1]


def slot_table(n_dp, d, s):
    orders = bit_orders(n_dp)
    core = s & 1
    entries = []
    for j in range(n_dp):
        rel = d ^ j
        for t in range(4):
            e = t // 2
            slot = core ^ e
            for bit in orders[e]:
                slot = slot * 2 + ((rel >> bit) & 1)
            entries.append(slot * 2 + t % 2)
    return jnp.stack(entries).astype(jnp.int32)


def reduce_units(units, n_dp, n_seq):
    orders = bit_orders(n_dp)
    flips = [lambda d, s: (d, s ^ 1)]
    for zero, one in zip(*orders):
        flips.append(
            lambda d, s, zero=zero, one=one: (d ^ (1 << (one if s & 1 else zero)), s)
        )
    for flip in flips:
        half = units.shape[0] // 2
        got = lax.ppermute(units[half:], BOTH, pairs(n_dp, n_seq, flip))
        units = (units[:half].astype(F32) + got.astype(F32)).astype(BF16)
    got = lax.ppermute(units, BOTH, pairs(n_dp, n_seq, lambda d, s: (d, s ^ 2)))
    units = (units.astype(F32) + got.astype(F32)).astype(BF16)
    other = lax.ppermute(units, BOTH, pairs(n_dp, n_seq, lambda d, s: (d, s ^ 1)))
    odd = (lax.axis_index("seq") & 1) == 1
    return jnp.concatenate(
        [jnp.where(odd, other, units), jnp.where(odd, units, other)], 0
    ).astype(F32)


def sum_all(values, n_dp, n_seq):
    for k in (1, 2):
        values = values + lax.ppermute(
            values, BOTH, pairs(n_dp, n_seq, lambda d, s, k=k: (d, s ^ k))
        )
    for bit in range(n_dp.bit_length() - 1):
        values = values + lax.ppermute(
            values, BOTH, pairs(n_dp, n_seq, lambda d, s, bit=bit: (d ^ (1 << bit), s))
        )
    return values


def unit_kernel(n_dp, split_rows, table, left, right, out):
    block = pl.program_id(0)
    full = lax.dot_general(
        left[...], right[...], (((0,), (0,)), ((), ())), preferred_element_type=F32
    ).astype(BF16)
    rows = full.shape[0] // n_dp
    for m in range(n_dp):
        if split_rows:
            unit = block * n_dp + m
        else:
            unit = m * 4 + block
        out[table[unit]] = full[m * rows : (m + 1) * rows]


def gradient_units(left, right, table, n_dp, split_rows):
    tokens = left.shape[0]
    width = 768
    rows = width // n_dp
    one = lambda b, t: (0, 0)
    piece = lambda b, t: (0, b)
    return pl.pallas_call(
        lambda *refs: unit_kernel(n_dp, split_rows, *refs),
        out_shape=jax.ShapeDtypeStruct((4 * n_dp, rows, width), BF16),
        grid_spec=pltpu.PrefetchScalarGridSpec(
            num_scalar_prefetch=1,
            grid=(4,),
            in_specs=[
                pl.BlockSpec((tokens, width), piece if left.shape[1] > width else one),
                pl.BlockSpec((tokens, width), piece if right.shape[1] > width else one),
            ],
            out_specs=pl.BlockSpec((4 * n_dp, rows, width), lambda b, t: (0, 0, 0)),
        ),
        compiler_params=pltpu.CompilerParams(vmem_limit_bytes=48 << 20),
        name="gradient_units",
    )(table, left, right)


def local(
    hidden_states,
    lengths,
    query_weight,
    query_bias,
    key_weight,
    value_weight,
    value_bias,
    out_weight,
    out_bias,
    attn_gain,
    attn_shift,
    inner_weight,
    inner_bias,
    outer_weight,
    outer_bias,
    ffn_gain,
    ffn_shift,
    cotangent,
):
    passages, slice_rows, width = hidden_states.shape
    n_seq = lax.axis_size("seq")
    n_dp = lax.axis_size("dp")
    d = lax.axis_index("dp")
    s = lax.axis_index("seq")
    tokens = slice_rows * n_seq
    heads = width // HEAD_DIM
    scale = 1.0 / math.sqrt(HEAD_DIM)
    table = slot_table(n_dp, d, s)

    def to_passage(values):
        blocks = exchange([pick(values, s ^ k) for k in range(n_seq)], n_seq)
        return jnp.concatenate(blocks, 0)

    def to_slots(values):
        values = values.reshape(n_seq, slice_rows, width)
        blocks = exchange([values[k] for k in range(n_seq)], n_seq)
        odd = (s & 1) == 1
        high = (s & 2) == 2
        low = [jnp.where(odd, blocks[k ^ 1], blocks[k]) for k in range(4)]
        return jnp.stack([jnp.where(high, low[k ^ 2], low[k]) for k in range(4)])

    def mm(left, right):
        return lax.dot_general(left, right, (((1,), (0,)), ((), ())), preferred_element_type=F32)

    def mm_t(left, right):
        return lax.dot_general(left, right, (((1,), (1,)), ((), ())), preferred_element_type=F32)

    tokens_in = to_passage(hidden_states)
    cot = to_passage(cotangent)
    length = pick(lengths, s)
    spots = lax.iota(jnp.int32, tokens)
    spots = ((spots // slice_rows) ^ s) * slice_rows + spots % slice_rows
    key_valid = (spots < length)[None, None, :]

    query = (mm(tokens_in, query_weight) + query_bias).astype(BF16)
    key = mm(tokens_in, key_weight).astype(BF16)
    value = (mm(tokens_in, value_weight) + value_bias).astype(BF16)

    def by_head(values):
        return values.reshape(tokens, heads, HEAD_DIM)

    def masked_scores():
        raw = jnp.einsum("qhd,khd->hqk", by_head(query), by_head(key), preferred_element_type=F32)
        return jnp.where(key_valid, raw * scale, MASKED)

    scores = masked_scores()
    row_top = jnp.max(scores, -1, keepdims=True)
    shifted_exp = jnp.exp(scores - row_top)
    row_total = jnp.sum(shifted_exp, -1, keepdims=True)
    log_total = row_top + jnp.log(row_total)
    probs = shifted_exp / row_total
    context = (
        jnp.einsum("hqk,khd->qhd", probs.astype(BF16), by_head(value), preferred_element_type=F32)
        .astype(BF16)
        .reshape(tokens, width)
    )
    attention = mm(context, out_weight) + out_bias
    residual_in = tokens_in.astype(F32) + attention
    normed, norm_one_pull = jax.vjp(layer_norm, residual_in, attn_gain, attn_shift)
    normed_low = normed.astype(BF16)
    inner_pre = mm(normed_low, inner_weight) + inner_bias
    activated, gelu_pull = jax.vjp(exact_gelu, inner_pre)
    activated_low = activated.astype(BF16)
    branch = mm(activated_low, outer_weight) + outer_bias
    block_result, norm_two_pull = jax.vjp(layer_norm, normed + branch, ffn_gain, ffn_shift)
    grad_pre, gain2, shift2 = norm_two_pull(cot.astype(F32))
    grad_branch = grad_pre.astype(BF16)
    outer_units = gradient_units(activated_low, grad_branch, table, n_dp, True)
    outer_sum = reduce_units(outer_units, n_dp, n_seq)
    block_output = to_slots(block_result.astype(BF16))
    fbias = jnp.sum(grad_branch, 0, dtype=F32)
    (grad_inner,) = gelu_pull(mm_t(grad_branch, outer_weight))
    inner_low = grad_inner.astype(BF16)
    inner_units = gradient_units(normed_low, inner_low, table, n_dp, False)
    inner_sum = reduce_units(inner_units, n_dp, n_seq)
    ibias = jnp.sum(inner_low, 0, dtype=F32)
    grad_normed = grad_pre + mm_t(inner_low, inner_weight)
    grad_mid, gain1, shift1 = norm_one_pull(grad_normed)
    grad_attn = grad_mid.astype(BF16)
    obias = jnp.sum(grad_attn, 0, dtype=F32)
    grad_context = mm_t(grad_attn, out_weight).astype(BF16)

    again = jnp.exp(masked_scores() - log_total)
    grad_value = (
        jnp.einsum("hqk,qhd->khd", again.astype(BF16), by_head(grad_context), preferred_element_type=F32)
        .astype(BF16)
        .reshape(tokens, width)
    )
    grad_probs = jnp.einsum(
        "qhd,khd->hqk", by_head(grad_context), by_head(value), preferred_element_type=F32
    )
    grad_scores = (again * (grad_probs - jnp.sum(again * grad_probs, -1, keepdims=True))).astype(BF16)
    grad_query = (
        (jnp.einsum("hqk,khd->qhd", grad_scores, by_head(key), preferred_element_type=F32) * scale)
        .astype(BF16)
        .reshape(tokens, width)
    )
    grad_key = (
        (jnp.einsum("hqk,qhd->khd", grad_scores, by_head(query), preferred_element_type=F32) * scale)
        .astype(BF16)
        .reshape(tokens, width)
    )
    stacked_left = jnp.concatenate([tokens_in, tokens_in, tokens_in, context], 1)
    stacked_right = jnp.concatenate([grad_query, grad_key, grad_value, grad_attn], 1)
    attn_units = gradient_units(stacked_left, stacked_right, table, n_dp, False)
    attn_sum = reduce_units(attn_units, n_dp, n_seq)
    qbias = jnp.sum(grad_query, 0, dtype=F32)
    vbias = jnp.sum(grad_value, 0, dtype=F32)
    input_grad = to_slots(
        (
            grad_mid
            + mm_t(grad_query, query_weight)
            + mm_t(grad_key, key_weight)
            + mm_t(grad_value, value_weight)
        ).astype(BF16)
    )
    vectors = jnp.stack([qbias, vbias, obias, gain1, shift1, fbias, gain2, shift2])
    vectors = sum_all(jnp.concatenate([vectors, ibias.reshape(4, width)], 0), n_dp, n_seq)
    part = width // n_dp
    mine = lax.dynamic_slice_in_dim(vectors[:8], d * part, part, 1)
    ibias_part = lax.dynamic_slice_in_dim(vectors[8:].reshape(4 * width), d * 4 * part, 4 * part, 0)
    return (
        block_output,
        input_grad,
        attn_sum[0],
        mine[0],
        attn_sum[1],
        attn_sum[2],
        mine[1],
        attn_sum[3],
        mine[2],
        mine[3],
        mine[4],
        jnp.concatenate([inner_sum[t] for t in range(4)], 1),
        ibias_part,
        outer_sum.reshape(4 * part, width),
        mine[5],
        mine[6],
        mine[7],
    )


def solution(mesh):
    tokens = P("dp", "seq", None)
    in_specs = (tokens, P("dp")) + (P(),) * 15 + (tokens,)
    rows = P("dp", None)
    vector = P("dp")
    out_specs = (
        tokens, tokens, rows, vector, rows, rows, vector, rows, vector,
        vector, vector, rows, vector, rows, vector, vector, vector,
    )
    return jax.shard_map(local, mesh=mesh, in_specs=in_specs, out_specs=out_specs, check_vma=False)
```

```python
import math

import jax
import jax.numpy as jnp
from jax import lax
from jax.experimental import pallas as pl
from jax.experimental.pallas import tpu as pltpu
from jax.sharding import PartitionSpec as P

HEAD_DIM = 64
EPSILON = 1e-12
MASKED = -1e30
BF16 = jnp.bfloat16
F32 = jnp.float32
BOTH = ("dp", "seq")


TAIL = (
    0.11283793300390244, 0.11283480376005173, 0.10392128676176071, 0.08427156507968903, 0.07071308046579361,
    -0.0027973579708486795, 0.08453421294689178, -0.0914449393749237, 0.025129476562142372,
)


def dot(left, right, contract=(1, 0)):
    return lax.dot_general(
        left, right, (((contract[0],), (contract[1],)), ((), ())), preferred_element_type=F32
    )


def gelu_and_slope(x):
    t = 1.0 / (1.0 + (0.4 / math.sqrt(2.0)) * jnp.abs(x))
    bell = jnp.exp(x * x * -0.5)
    poly = TAIL[-1]
    for c in TAIL[-2::-1]:
        poly = poly * t + c
    tail = poly * t * bell
    cdf = jnp.where(x < 0.0, tail, 1.0 - tail)
    return x * cdf, cdf + x * bell * (1.0 / math.sqrt(2.0 * math.pi))


def normalize(z):
    center = z - jnp.mean(z, -1, keepdims=True)
    r = lax.rsqrt(jnp.mean(center * center, -1, keepdims=True) + EPSILON)
    return center * r, r


def norm_back(c, n, r):
    return r * (c - jnp.mean(c, -1, keepdims=True) - n * jnp.mean(c * n, -1, keepdims=True))


def fold8(x):
    return jnp.sum(x.reshape(x.shape[0] // 8, 8, x.shape[1]), 0)


def put_units(keep, send, slots, base, full, which, cols=slice(None)):
    n_dp = keep.shape[0]
    h = keep.shape[2]
    odd = slots[0] == 1
    low = full.astype(BF16)
    for m in range(full.shape[0] // (2 * h)):
        first = low[2 * m * h : (2 * m + 1) * h]
        second = low[(2 * m + 1) * h : (2 * m + 2) * h]
        keep[slots[1 + base + m], which, :, cols] = jnp.where(odd, second, first)
        send[slots[1 + n_dp + base + m], which, :, cols] = jnp.where(odd, first, second)


def up_kernel(ROWS, slots, hat, gain1, shift1, wi, bi, wo, bo, gain2, shift2, cot,
              result, slope, gpre, vec, keep, send, act_s, low_s, acc_s, gb_s):
    f = pl.program_id(0)
    nf = act_s.shape[0]
    tokens = hat.shape[0]

    @pl.when(f == 0)
    def _():
        normed = hat[...] * gain1[...] + shift1[...]
        low_s[...] = normed.astype(BF16)
        acc_s[...] = normed + bo[...]

    @pl.when(f < nf)
    def _():
        for r in range(0, tokens, ROWS):
            rows = slice(r, r + ROWS)
            act, slow = gelu_and_slope(dot(low_s[rows], wi[...]) + bi[...])
            act = act.astype(BF16)
            act_s[f, rows] = act
            slope[rows] = slow.astype(BF16)
            acc_s[rows] += dot(act, wo[...])

    @pl.when(f == nf - 1)
    def _():
        step = 32

        def body(i, sums):
            rows = pl.ds(pl.multiple_of(i * step, step), step)
            n, r = normalize(acc_s[rows])
            result[rows] = (n * gain2[...] + shift2[...]).astype(BF16)
            g = cot[rows].astype(F32)
            gz = norm_back(g * gain2[...], n, r)
            gpre[rows] = gz
            low = gz.astype(BF16)
            gb_s[rows] = low
            return sums[0] + fold8(low.astype(F32)), sums[1] + fold8(g * n), sums[2] + fold8(g)

        zero = jnp.zeros((8, hat.shape[1]), F32)
        sums = lax.fori_loop(0, tokens // step, body, (zero, zero, zero))
        for k in range(3):
            vec[k : k + 1] = jnp.sum(sums[k], 0, keepdims=True)

    @pl.when(f >= nf)
    def _():
        blocks = keep.shape[0] // nf
        put_units(keep, send, slots, (f - nf) * blocks, dot(act_s[f - nf], gb_s[...], (0, 0)), 0)


def whole(shape):
    return pl.BlockSpec(shape, lambda *_: (0,) * len(shape))


def ffn_up(n_dp, slots, hat, gain1, shift1, wi, bi, wo, bo, gain2, shift2, cot, ROWS=128):
    tokens, width = hat.shape
    ff = wi.shape[1]
    nf = ff // width
    half = ff // (2 * n_dp)
    step = lambda f: jnp.minimum(f, nf - 1)
    vector = whole((1, width))
    return pl.pallas_call(
        lambda *refs: up_kernel(ROWS, *refs),
        out_shape=(
            jax.ShapeDtypeStruct((tokens, width), BF16),
            jax.ShapeDtypeStruct((tokens, ff), BF16),
            jax.ShapeDtypeStruct((tokens, width), F32),
            jax.ShapeDtypeStruct((8, width), F32),
            jax.ShapeDtypeStruct((n_dp, 1, half, width), BF16),
            jax.ShapeDtypeStruct((n_dp, 1, half, width), BF16),
        ),
        grid_spec=pltpu.PrefetchScalarGridSpec(
            num_scalar_prefetch=1,
            grid=(2 * nf,),
            in_specs=[
                whole((tokens, width)), vector, vector,
                pl.BlockSpec((width, width), lambda f, s: (0, step(f))),
                pl.BlockSpec((1, width), lambda f, s: (0, step(f))),
                pl.BlockSpec((width, width), lambda f, s: (step(f), 0)),
                vector, vector, vector, whole((tokens, width)),
            ],
            out_specs=[
                whole((tokens, width)),
                pl.BlockSpec((tokens, width), lambda f, s: (0, step(f))),
                whole((tokens, width)),
                whole((8, width)),
                whole((n_dp, 1, half, width)),
                whole((n_dp, 1, half, width)),
            ],
            scratch_shapes=[
                pltpu.VMEM((nf, tokens, width), BF16),
                pltpu.VMEM((tokens, width), BF16),
                pltpu.VMEM((tokens, width), F32),
                pltpu.VMEM((tokens, width), BF16),
            ],
        ),
        compiler_params=pltpu.CompilerParams(vmem_limit_bytes=58 << 20),
        name="ffn_up",
    )(slots, hat, gain1, shift1, wi, bi, wo, bo, gain2, shift2, cot)


def attn_kernel(ROWS, x, bias, wq, bq, wk, wv, bv, wo, bo, q_out, k_out, v_out, p_out, c_out, hat_out, r_out, acc_s):
    g = pl.program_id(0)
    tokens = x.shape[0]
    xs = x[...]
    qs = (dot(xs, wq[...]) + bq[...]).astype(BF16) * (1.0 / math.sqrt(HEAD_DIM))
    ks = dot(xs, wk[...]).astype(BF16)
    vs = (dot(xs, wv[...]) + bv[...]).astype(BF16)
    q_out[...] = qs
    k_out[...] = ks
    v_out[...] = vs
    lane = lax.broadcasted_iota(jnp.int32, (1, 2 * HEAD_DIM), 1) < HEAD_DIM
    nil = jnp.zeros((), BF16)
    for pair in range(qs.shape[1] // (2 * HEAD_DIM)):
        cols = slice(pair * 2 * HEAD_DIM, (pair + 1) * 2 * HEAD_DIM)
        q2, k2, v2 = qs[:, cols], ks[:, cols], vs[:, cols]
        mine = (lane, jnp.logical_not(lane))
        vm = [jnp.where(m, v2, nil) for m in mine]
        for r in range(0, tokens, ROWS):
            rows = slice(r, r + ROWS)
            total = None
            for h in range(2):
                s = dot(jnp.where(mine[h], q2[rows], nil), k2, (1, 1)) + bias[...]
                e = jnp.exp(s - jnp.max(s, -1, keepdims=True))
                p = (e * (1.0 / jnp.sum(e, -1, keepdims=True))).astype(BF16)
                p_out[pair * 2 + h, rows] = p
                part = dot(p, vm[h])
                total = part if total is None else total + part
            c_out[rows, cols] = total.astype(BF16)
    more = dot(c_out[...], wo[...])

    @pl.when(g == 0)
    def _():
        acc_s[...] = xs.astype(F32) + bo[...] + more

    @pl.when(g > 0)
    def _():
        acc_s[...] += more

    @pl.when(g == pl.num_programs(0) - 1)
    def _():
        step = 32

        def body(i, _):
            rows = pl.ds(pl.multiple_of(i * step, step), step)
            n, r = normalize(acc_s[rows])
            hat_out[rows] = n
            r_out[rows] = r
            return 0

        lax.fori_loop(0, tokens // step, body, 0)


def attention_forward(x, bias, wq, bq, wk, wv, bv, wo, bo, ROWS=128):
    tokens, width = x.shape
    group = 4 * HEAD_DIM
    n = width // group
    heads = width // HEAD_DIM
    col = lambda rows: pl.BlockSpec((rows, group), lambda g: (0, g))
    low = jax.ShapeDtypeStruct((tokens, width), BF16)
    return pl.pallas_call(
        lambda *refs: attn_kernel(ROWS, *refs),
        out_shape=(
            low, low, low,
            jax.ShapeDtypeStruct((heads, tokens, tokens), BF16),
            low,
            jax.ShapeDtypeStruct((tokens, width), F32),
            jax.ShapeDtypeStruct((tokens, 1), F32),
        ),
        grid=(n,),
        in_specs=[
            whole((tokens, width)), whole((1, tokens)),
            col(width), col(1), col(width), col(width), col(1),
            pl.BlockSpec((group, width), lambda g: (g, 0)), whole((1, width)),
        ],
        out_specs=[
            col(tokens), col(tokens), col(tokens),
            pl.BlockSpec((4, tokens, tokens), lambda g: (g, 0, 0)),
            col(tokens), whole((tokens, width)), whole((tokens, 1)),
        ],
        scratch_shapes=[pltpu.VMEM((tokens, width), F32)],
        compiler_params=pltpu.CompilerParams(vmem_limit_bytes=58 << 20),
        name="attention_forward",
    )(x, bias, wq, bq, wk, wv, bv, wo, bo)


def down_kernel(ROWS, slots, gpre, slope, hat, gain1, shift1, wo, gi, ibias, keep, send, gb_s, nt_s):
    f = pl.program_id(0)
    tokens, width = hat.shape

    @pl.when(f == 0)
    def _():
        gb_s[...] = gpre[...].astype(BF16)
        nt_s[...] = (hat[...] * gain1[...] + shift1[...]).astype(BF16).T

    sums = jnp.zeros((8, width), F32)
    for r in range(0, tokens, ROWS):
        rows = slice(r, r + ROWS)
        low = (dot(gb_s[rows], wo[...], (1, 1)) * slope[rows].astype(F32)).astype(BF16)
        gi[rows] = low
        sums = sums + fold8(low.astype(F32))
    ibias[...] = jnp.sum(sums, 0, keepdims=True)
    put_units(keep, send, slots, 0, dot(nt_s[...], gi[...]), f)


def ffn_down(n_dp, slots, gpre, slope, hat, gain1, shift1, wo, ROWS=128):
    tokens, width = hat.shape
    ff = wo.shape[0]
    nf = ff // width
    vector = whole((1, width))
    full = whole((tokens, width))
    piece = pl.BlockSpec((tokens, width), lambda f, s: (0, f))
    shape = (n_dp, nf, width // (2 * n_dp), width)
    units = jax.ShapeDtypeStruct(shape, BF16)
    return pl.pallas_call(
        lambda *refs: down_kernel(ROWS, *refs),
        out_shape=(
            jax.ShapeDtypeStruct((tokens, ff), BF16),
            jax.ShapeDtypeStruct((1, ff), F32),
            units, units,
        ),
        grid_spec=pltpu.PrefetchScalarGridSpec(
            num_scalar_prefetch=1,
            grid=(nf,),
            in_specs=[
                full, piece, full, vector, vector,
                pl.BlockSpec((width, width), lambda f, s: (f, 0)),
            ],
            out_specs=[
                piece,
                pl.BlockSpec((1, width), lambda f, s: (0, f)),
                whole(shape), whole(shape),
            ],
            scratch_shapes=[
                pltpu.VMEM((tokens, width), BF16),
                pltpu.VMEM((width, tokens), BF16),
            ],
        ),
        compiler_params=pltpu.CompilerParams(vmem_limit_bytes=58 << 20),
        name="ffn_down",
    )(slots, gpre, slope, hat, gain1, shift1, wo)


def mid_kernel(slots, gpre, gi, hat, r1, gain1, wi, wa, ctx, gmid, gctx, vec, keep, send, acc_s, gb_s):
    f = pl.program_id(0)
    tokens, width = hat.shape
    more = dot(gi[...], wi[...], (1, 1))

    @pl.when(f == 0)
    def _():
        acc_s[...] = gpre[...] + more

    @pl.when(f > 0)
    def _():
        acc_s[...] += more

    @pl.when(f == pl.num_programs(0) - 1)
    def _():
        step = 32

        def body(i, sums):
            rows = pl.ds(pl.multiple_of(i * step, step), step)
            n = hat[rows]
            g = acc_s[rows]
            gz = norm_back(g * gain1[...], n, r1[rows])
            gmid[rows] = gz
            low = gz.astype(BF16)
            gb_s[rows] = low
            return sums[0] + fold8(low.astype(F32)), sums[1] + fold8(g * n), sums[2] + fold8(g)

        zero = jnp.zeros((8, width), F32)
        sums = lax.fori_loop(0, tokens // step, body, (zero, zero, zero))
        for k in range(3):
            vec[k : k + 1] = jnp.sum(sums[k], 0, keepdims=True)
        gctx[...] = dot(gb_s[...], wa[...], (1, 1)).astype(BF16)
        put_units(keep, send, slots, 0, dot(ctx[...].T, gb_s[...]), 0)


def middle(n_dp, slots, gpre, gi, hat, r1, gain1, wi, wa, ctx):
    tokens, width = hat.shape
    nf = wi.shape[1] // width
    full = whole((tokens, width))
    shape = (n_dp, 1, width // (2 * n_dp), width)
    units = jax.ShapeDtypeStruct(shape, BF16)
    return pl.pallas_call(
        mid_kernel,
        out_shape=(
            jax.ShapeDtypeStruct((tokens, width), F32),
            jax.ShapeDtypeStruct((tokens, width), BF16),
            jax.ShapeDtypeStruct((8, width), F32),
            units, units,
        ),
        grid_spec=pltpu.PrefetchScalarGridSpec(
            num_scalar_prefetch=1,
            grid=(nf,),
            in_specs=[
                full,
                pl.BlockSpec((tokens, width), lambda f, s: (0, f)),
                full, whole((tokens, 1)), whole((1, width)),
                pl.BlockSpec((width, width), lambda f, s: (0, f)),
                whole((width, width)), full,
            ],
            out_specs=[full, full, whole((8, width)), whole(shape), whole(shape)],
            scratch_shapes=[pltpu.VMEM((tokens, width), F32), pltpu.VMEM((tokens, width), BF16)],
        ),
        compiler_params=pltpu.CompilerParams(vmem_limit_bytes=58 << 20),
        name="middle",
    )(slots, gpre, gi, hat, r1, gain1, wi, wa, ctx)


def back_kernel(
    ROWS, slots, x, q, k, v, c, gc, p, dq, dk, dv, qb, vb, keep, send, xt_s, ds_s
):
    g = pl.program_id(0)
    tokens = x.shape[0]
    scale = 1.0 / math.sqrt(HEAD_DIM)
    pair_width = 2 * HEAD_DIM

    @pl.when(g == 0)
    def _():
        xt_s[...] = x[...].T

    lane = lax.broadcasted_iota(jnp.int32, (1, pair_width), 1) < HEAD_DIM
    mine = (lane, jnp.logical_not(lane))
    nil = jnp.zeros((), BF16)
    for pair in range(q.shape[1] // pair_width):
        cols = slice(pair * pair_width, (pair + 1) * pair_width)
        q2, k2, v2, c2, g2 = q[:, cols], k[:, cols], v[:, cols], c[:, cols], gc[:, cols]
        qt, gt = q2.T, g2.T
        prod = g2.astype(F32) * c2.astype(F32)
        dkt, dvt = [], []
        for r in range(0, tokens, ROWS):
            rows = slice(r, r + ROWS)
            total = None
            for h in range(2):
                delta = jnp.sum(jnp.where(mine[h], prod[rows], 0.0), -1, keepdims=True)
                dp = dot(jnp.where(mine[h], g2[rows], nil), v2, (1, 1))
                ds = (p[pair * 2 + h, rows].astype(F32) * (dp - delta)).astype(BF16)
                ds_s[h, rows] = ds
                part = dot(ds, jnp.where(mine[h], k2, nil))
                total = part if total is None else total + part
            dq[rows, cols] = (total * scale).astype(BF16)
        for h in range(2):
            rows = slice(h * HEAD_DIM, (h + 1) * HEAD_DIM)
            dvt.append(dot(gt[rows], p[pair * 2 + h]))
            dkt.append(dot(qt[rows], ds_s[h]))
        dv[:, cols] = jnp.concatenate(dvt, 0).astype(BF16).T
        dk[:, cols] = jnp.concatenate(dkt, 0).astype(BF16).T
    qb[...] = jnp.sum(fold8(dq[...].astype(F32)), 0, keepdims=True)
    vb[...] = jnp.sum(fold8(dv[...].astype(F32)), 0, keepdims=True)
    width = q.shape[1]
    cols = pl.ds(pl.multiple_of(g * width, width), width)
    for n, grad in enumerate((dq, dk, dv)):
        put_units(keep, send, slots, 0, dot(xt_s[...], grad[...]), n, cols)


def attention_back(n_dp, slots, x, q, k, v, c, gc, p, ROWS=128):
    tokens, width = x.shape
    group = 4 * HEAD_DIM
    col = pl.BlockSpec((tokens, group), lambda g, s: (0, g))
    row = pl.BlockSpec((1, group), lambda g, s: (0, g))
    low = jax.ShapeDtypeStruct((tokens, width), BF16)
    vector = jax.ShapeDtypeStruct((1, width), F32)
    shape = (n_dp, 3, width // (2 * n_dp), width)
    units = jax.ShapeDtypeStruct(shape, BF16)
    return pl.pallas_call(
        lambda *refs: back_kernel(ROWS, *refs),
        out_shape=(low, low, low, vector, vector, units, units),
        grid_spec=pltpu.PrefetchScalarGridSpec(
            num_scalar_prefetch=1,
            grid=(width // group,),
            in_specs=[whole((tokens, width)), col, col, col, col, col,
                      pl.BlockSpec((4, tokens, tokens), lambda g, s: (g, 0, 0))],
            out_specs=[col, col, col, row, row, whole(shape), whole(shape)],
            scratch_shapes=[
                pltpu.VMEM((width, tokens), BF16),
                pltpu.VMEM((2, tokens, tokens), BF16),
            ],
        ),
        compiler_params=pltpu.CompilerParams(vmem_limit_bytes=58 << 20),
        name="attention_back",
    )(slots, x, q, k, v, c, gc, p)


def input_kernel(gmid, dq, dk, dv, wq, wk, wv, out):
    total = gmid[...] + dot(dq[...], wq[...], (1, 1))
    total = total + dot(dk[...], wk[...], (1, 1))
    out[...] = (total + dot(dv[...], wv[...], (1, 1))).astype(BF16)


def input_gradient(gmid, dq, dk, dv, wq, wk, wv):
    tokens, width = gmid.shape
    rows = tokens // 4
    act = pl.BlockSpec((rows, width), lambda i: (i, 0))
    weight = whole((width, width))
    return pl.pallas_call(
        input_kernel,
        out_shape=jax.ShapeDtypeStruct((tokens, width), BF16),
        grid=(4,),
        in_specs=[act, act, act, act, weight, weight, weight],
        out_specs=act,
        compiler_params=pltpu.CompilerParams(vmem_limit_bytes=58 << 20),
        name="input_gradient",
    )(gmid, dq, dk, dv, wq, wk, wv)


def pairs(n_dp, n_seq, partner):
    out = []
    for d in range(n_dp):
        for s in range(n_seq):
            e, t = partner(d, s)
            out.append((d * n_seq + s, e * n_seq + t))
    return out


def pick(blocks, index):
    return lax.dynamic_index_in_dim(blocks, index, 0, keepdims=False)


def after(values, *others):
    return lax.optimization_barrier((values, others))[0]


def exchange(blocks, n_seq):
    return [blocks[0]] + [
        lax.ppermute(blocks[k], "seq", [(s, s ^ k) for s in range(n_seq)]) for k in range(1, n_seq)
    ]


def bit_orders(n_dp):
    bits = list(range(n_dp.bit_length() - 1))
    return bits, bits[1:] + bits[:1]


def slot_table(n_dp, d, s):
    orders = bit_orders(n_dp)
    odd = (s & 1) == 1
    by_core = []
    for order in orders:
        entries = []
        for j in range(n_dp):
            slot = 0
            for bit in order:
                slot = slot * 2 + (((d ^ j) >> bit) & 1)
            entries.append(slot)
        by_core.append(jnp.stack(entries))
    kept = jnp.where(odd, by_core[1], by_core[0])
    sent = jnp.where(odd, by_core[0], by_core[1])
    return jnp.concatenate([(s & 1)[None], kept, sent]).astype(jnp.int32)


def added(pieces, cut):
    total = pieces[0][cut].astype(F32)
    for piece in pieces[1:]:
        total = total + piece[cut].astype(F32)
    return total.astype(BF16)


class Halving:
    def __init__(self, keep, send, n_dp, n_seq):
        self.n_dp = n_dp
        self.n_seq = n_seq
        self.flips = [
            lambda d, s, zero=zero, one=one: (d ^ (1 << (one if s & 1 else zero)), s)
            for zero, one in zip(*bit_orders(n_dp))
        ]
        self.families = [[keep, self.permute(send, lambda d, s: (d, s ^ 1))]]

    def permute(self, values, partner):
        return lax.ppermute(values, BOTH, pairs(self.n_dp, self.n_seq, partner))

    def join(self, other):
        self.families += other.families

    def sums(self, cut):
        return jnp.concatenate([added(pieces, cut) for pieces in self.families], 1)

    def step(self, *wait):
        half = self.families[0][0].shape[0] // 2
        send = self.sums(slice(half, None))
        got = self.permute(after(send, *wait) if wait else send, self.flips.pop(0))
        families, first = [], 0
        for pieces in self.families:
            n = pieces[0].shape[1]
            families.append([piece[:half] for piece in pieces] + [got[:, first : first + n]])
            first += n
        self.families = families
        return got

    def share_y(self):
        mine = self.sums(slice(None))[0]
        got = self.permute(mine, lambda d, s: (d, s ^ 2))
        self.mine = (mine.astype(F32) + got.astype(F32)).astype(BF16)
        return got

    def share_core(self):
        other = self.permute(self.mine, lambda d, s: (d, s ^ 1))
        odd = (lax.axis_index("seq") & 1) == 1
        first = jnp.where(odd, other, self.mine)
        second = jnp.where(odd, self.mine, other)
        return jnp.concatenate([first, second], 1).astype(F32)


def sum_all(values, n_dp, n_seq):
    flips = [lambda d, s, k=k: (d, s ^ k) for k in (1, 2)]
    for bit in range(n_dp.bit_length() - 1):
        flips.append(lambda d, s, bit=bit: (d ^ (1 << bit), s))
    for flip in flips:
        values = values + lax.ppermute(values, BOTH, pairs(n_dp, n_seq, flip))
    return values


def local(
    hidden_states,
    lengths,
    query_weight,
    query_bias,
    key_weight,
    value_weight,
    value_bias,
    out_weight,
    out_bias,
    attn_gain,
    attn_shift,
    inner_weight,
    inner_bias,
    outer_weight,
    outer_bias,
    ffn_gain,
    ffn_shift,
    cotangent,
):
    _, slice_rows, width = hidden_states.shape
    n_seq = lax.axis_size("seq")
    n_dp = lax.axis_size("dp")
    d = lax.axis_index("dp")
    s = lax.axis_index("seq")
    tokens = slice_rows * n_seq
    slots = slot_table(n_dp, d, s)

    def to_passage(values):
        blocks = exchange([pick(values, s ^ k) for k in range(n_seq)], n_seq)
        return jnp.concatenate(blocks, 0)

    def to_slots(values):
        values = values.reshape(n_seq, slice_rows, width)
        blocks = exchange([values[k] for k in range(n_seq)], n_seq)
        odd = (s & 1) == 1
        high = (s & 2) == 2
        low = [jnp.where(odd, blocks[k ^ 1], blocks[k]) for k in range(4)]
        return jnp.stack([jnp.where(high, low[k ^ 2], low[k]) for k in range(4)])

    def row(vector):
        return vector.reshape(1, -1)

    x = to_passage(hidden_states)
    cot = to_passage(after(cotangent, x))
    spots = lax.iota(jnp.int32, tokens)
    spots = ((spots // slice_rows) ^ s) * slice_rows + spots % slice_rows
    bias = row(jnp.where(spots < pick(lengths, s), 0.0, MASKED))

    query, key, value, probs, context, hat, r1 = attention_forward(
        x, bias, query_weight, row(query_bias), key_weight, value_weight, row(value_bias),
        out_weight, row(out_bias),
    )
    gain1, shift1 = row(attn_gain), row(attn_shift)
    result, slope, grad_pre, vec2, *outer_units = ffn_up(
        n_dp, slots, hat, gain1, shift1, inner_weight, row(inner_bias), outer_weight,
        row(outer_bias), row(ffn_gain), row(ffn_shift), cot,
    )
    outer = Halving(*outer_units, n_dp, n_seq)
    grad_inner, ibias, *inner_units = ffn_down(
        n_dp, slots, grad_pre, slope, hat, gain1, shift1, outer_weight
    )
    inner = Halving(*inner_units, n_dp, n_seq)
    a1 = outer.step()
    grad_mid, grad_context, vec1, *out_units = middle(
        n_dp, slots, grad_pre, grad_inner, hat, r1, gain1, inner_weight, out_weight, context,
    )
    inner.join(Halving(*out_units, n_dp, n_seq))
    a2 = outer.step()
    b1 = inner.step()
    grad_query, grad_key, grad_value, qbias, vbias, *attn_units = attention_back(
        n_dp, slots, x, query, key, value, context, grad_context, probs,
    )
    attn = Halving(*attn_units, n_dp, n_seq)
    input_low = input_gradient(
        grad_mid, grad_query, grad_key, grad_value, query_weight, key_weight, value_weight,
    )
    vectors = jnp.concatenate([vec2[:3], vec1[:3], qbias, vbias, ibias.reshape(4, width)], 0)
    c1 = attn.step()
    b2 = inner.step()
    a3 = outer.step()
    c2 = attn.step()
    b3 = inner.step()
    outer.share_y()
    c3 = attn.step()
    while attn.flips:
        attn.step()
        inner.step()
        outer.step()
    inner.share_y()
    attn.share_y()
    vectors = sum_all(vectors, n_dp, n_seq)
    block_output = to_slots(result)
    input_grad = to_slots(input_low)
    outer_sum = outer.share_core()
    inner_sum = inner.share_core()
    attn_sum = attn.share_core()
    part = width // n_dp
    mine = lax.dynamic_slice_in_dim(vectors[:8], d * part, part, 1)
    ibias_part = lax.dynamic_slice_in_dim(vectors[8:].reshape(4 * width), d * 4 * part, 4 * part, 0)
    return (
        block_output,
        input_grad,
        attn_sum[0],
        mine[6],
        attn_sum[1],
        attn_sum[2],
        mine[7],
        inner_sum[4],
        mine[3],
        mine[4],
        mine[5],
        jnp.concatenate([inner_sum[t] for t in range(4)], 1),
        ibias_part,
        outer_sum[0],
        mine[0],
        mine[1],
        mine[2],
    )


def solution(mesh):
    tokens = P("dp", "seq", None)
    in_specs = (tokens, P("dp")) + (P(),) * 15 + (tokens,)
    rows = P("dp", None)
    vector = P("dp")
    out_specs = (
        tokens, tokens, rows, vector, rows, rows, vector, rows, vector,
        vector, vector, rows, vector, rows, vector, vector, vector,
    )
    return jax.shard_map(local, mesh=mesh, in_specs=in_specs, out_specs=out_specs, check_vma=False)
```

```python
import math

import jax
import jax.numpy as jnp
from jax import lax
from jax.experimental import pallas as pl
from jax.experimental.pallas import tpu as pltpu
from jax.sharding import PartitionSpec as P

HEAD_DIM = 64
EPSILON = 1e-12
MASKED = -1e30
BF16 = jnp.bfloat16
F32 = jnp.float32
BOTH = ("dp", "seq")


LN_ROWS = 256

TAIL = (
    0.11283793300390244, 0.11283480376005173, 0.10392128676176071, 0.08427156507968903, 0.07071308046579361,
    -0.0027973579708486795, 0.08453421294689178, -0.0914449393749237, 0.025129476562142372,
)


def dot(left, right, contract=(1, 0)):
    return lax.dot_general(
        left, right, (((contract[0],), (contract[1],)), ((), ())), preferred_element_type=F32
    )


def gelu_and_slope(x):
    t = 1.0 / (1.0 + (0.4 / math.sqrt(2.0)) * jnp.abs(x))
    bell = jnp.exp2(x * x * (-0.5 * math.log2(math.e)))
    poly = TAIL[-1]
    for c in TAIL[-2::-1]:
        poly = poly * t + c
    tail = poly * t * bell
    cdf = jnp.where(x < 0.0, tail, 1.0 - tail)
    return x * cdf, cdf + x * bell * (1.0 / math.sqrt(2.0 * math.pi))


def normalize(z):
    center = z - jnp.mean(z, -1, keepdims=True)
    r = lax.rsqrt(jnp.mean(center * center, -1, keepdims=True) + EPSILON)
    return center * r, r


def norm_back(c, n, r):
    return r * (c - jnp.mean(c, -1, keepdims=True) - n * jnp.mean(c * n, -1, keepdims=True))


def fold8(x):
    return jnp.sum(x.reshape(x.shape[0] // 8, 8, x.shape[1]), 0)


def put_units(keep, send, slots, base, full, which, cols=slice(None)):
    n_dp = keep.shape[0]
    h = keep.shape[2]
    odd = slots[0] == 1
    low = full.astype(BF16)
    for m in range(full.shape[0] // (2 * h)):
        first = low[2 * m * h : (2 * m + 1) * h]
        second = low[(2 * m + 1) * h : (2 * m + 2) * h]
        keep[slots[1 + base + m], which, :, cols] = jnp.where(odd, second, first)
        send[slots[1 + n_dp + base + m], which, :, cols] = jnp.where(odd, first, second)


def up_kernel(ROWS, slots, hat, gain1, shift1, wi, bi, wo, bo, gain2, shift2, cot,
              result, slope, gpre, vec, keep, send, act_s, low_s, acc_s, gb_s):
    f = pl.program_id(0)
    nf = act_s.shape[0]
    tokens = hat.shape[0]

    @pl.when(f == 0)
    def _():
        normed = hat[...] * gain1[...] + shift1[...]
        low_s[...] = normed.astype(BF16)
        acc_s[...] = normed + bo[...]

    @pl.when(f < nf)
    def _():
        for r in range(0, tokens, ROWS):
            rows = slice(r, r + ROWS)
            act, slow = gelu_and_slope(dot(low_s[rows], wi[...]) + bi[...])
            act = act.astype(BF16)
            act_s[f, rows] = act
            slope[rows] = slow.astype(BF16)
            acc_s[rows] += dot(act, wo[...])

    @pl.when(f == nf - 1)
    def _():
        step = LN_ROWS

        def body(i, sums):
            rows = pl.ds(pl.multiple_of(i * step, step), step)
            n, r = normalize(acc_s[rows])
            result[rows] = (n * gain2[...] + shift2[...]).astype(BF16)
            g = cot[rows].astype(F32)
            gz = norm_back(g * gain2[...], n, r)
            gpre[rows] = gz
            low = gz.astype(BF16)
            gb_s[rows] = low
            return sums[0] + fold8(low.astype(F32)), sums[1] + fold8(g * n), sums[2] + fold8(g)

        zero = jnp.zeros((8, hat.shape[1]), F32)
        sums = lax.fori_loop(0, tokens // step, body, (zero, zero, zero))
        for k in range(3):
            vec[k : k + 1] = jnp.sum(sums[k], 0, keepdims=True)

    @pl.when(f >= nf)
    def _():
        blocks = keep.shape[0] // nf
        put_units(keep, send, slots, (f - nf) * blocks, dot(act_s[f - nf], gb_s[...], (0, 0)), 0)


def whole(shape):
    return pl.BlockSpec(shape, lambda *_: (0,) * len(shape))


def ffn_up(n_dp, slots, hat, gain1, shift1, wi, bi, wo, bo, gain2, shift2, cot, ROWS=512):
    tokens, width = hat.shape
    ff = wi.shape[1]
    nf = ff // width
    half = ff // (2 * n_dp)
    step = lambda f: jnp.minimum(f, nf - 1)
    vector = whole((1, width))
    return pl.pallas_call(
        lambda *refs: up_kernel(ROWS, *refs),
        out_shape=(
            jax.ShapeDtypeStruct((tokens, width), BF16),
            jax.ShapeDtypeStruct((tokens, ff), BF16),
            jax.ShapeDtypeStruct((tokens, width), F32),
            jax.ShapeDtypeStruct((8, width), F32),
            jax.ShapeDtypeStruct((n_dp, 1, half, width), BF16),
            jax.ShapeDtypeStruct((n_dp, 1, half, width), BF16),
        ),
        grid_spec=pltpu.PrefetchScalarGridSpec(
            num_scalar_prefetch=1,
            grid=(2 * nf,),
            in_specs=[
                whole((tokens, width)), vector, vector,
                pl.BlockSpec((width, width), lambda f, s: (0, step(f))),
                pl.BlockSpec((1, width), lambda f, s: (0, step(f))),
                pl.BlockSpec((width, width), lambda f, s: (step(f), 0)),
                vector, vector, vector, whole((tokens, width)),
            ],
            out_specs=[
                whole((tokens, width)),
                pl.BlockSpec((tokens, width), lambda f, s: (0, step(f))),
                whole((tokens, width)),
                whole((8, width)),
                whole((n_dp, 1, half, width)),
                whole((n_dp, 1, half, width)),
            ],
            scratch_shapes=[
                pltpu.VMEM((nf, tokens, width), BF16),
                pltpu.VMEM((tokens, width), BF16),
                pltpu.VMEM((tokens, width), F32),
                pltpu.VMEM((tokens, width), BF16),
            ],
        ),
        compiler_params=pltpu.CompilerParams(vmem_limit_bytes=20 << 20),
        name="ffn_up",
    )(slots, hat, gain1, shift1, wi, bi, wo, bo, gain2, shift2, cot)


def attn_kernel(x, bias, wq, bq, wk, wv, bv, wo, bo,
                q_out, k_out, v_out, e_out, inv_out, c_out, hat_out, r_out, acc_s):
    g = pl.program_id(0)
    tokens = x.shape[0]
    xs = x[...]
    qs = (dot(xs, wq[...]) + bq[...]).astype(BF16) * (1.0 / math.sqrt(HEAD_DIM))
    ks = dot(xs, wk[...]).astype(BF16)
    vs = (dot(xs, wv[...]) + bv[...]).astype(BF16)
    q_out[...] = qs
    k_out[...] = ks
    v_out[...] = vs
    lanes = lax.broadcasted_iota(jnp.int32, (1, 2 * HEAD_DIM), 1)
    low = lanes < HEAD_DIM
    mine = (low, jnp.logical_not(low))
    nil = jnp.zeros((), BF16)
    one = jnp.ones((), BF16)
    for pair in range(qs.shape[1] // (2 * HEAD_DIM)):
        cols = slice(pair * 2 * HEAD_DIM, (pair + 1) * 2 * HEAD_DIM)
        q2, k2, v2 = qs[:, cols], ks[:, cols], vs[:, cols]
        sums = []
        for h in range(2):
            spare = lanes == (HEAD_DIM if h == 0 else 0)
            qa = jnp.where(mine[h], q2, jnp.where(spare, one, nil))
            ka = jnp.where(mine[h], k2, jnp.where(spare, bias[...], nil))
            s = dot(qa, ka, (1, 1))
            e = jnp.exp(s - jnp.max(s, -1, keepdims=True)).astype(BF16)
            e_out[pair * 2 + h] = e
            sums.append(dot(e, jnp.where(mine[h], v2, one)))
        inv = 1.0 / pltpu.roll(jnp.where(low, sums[1], sums[0]), HEAD_DIM, 1)
        inv_out[:, cols] = inv
        c_out[:, cols] = (jnp.where(low, sums[0], sums[1]) * inv).astype(BF16)
    more = dot(c_out[...], wo[...])

    @pl.when(g == 0)
    def _():
        acc_s[...] = xs.astype(F32) + bo[...] + more

    @pl.when(g > 0)
    def _():
        acc_s[...] += more

    @pl.when(g == pl.num_programs(0) - 1)
    def _():
        step = LN_ROWS

        def body(i, _):
            rows = pl.ds(pl.multiple_of(i * step, step), step)
            n, r = normalize(acc_s[rows])
            hat_out[rows] = n
            r_out[rows] = r
            return 0

        lax.fori_loop(0, tokens // step, body, 0)


def attention_forward(x, bias, wq, bq, wk, wv, bv, wo, bo):
    tokens, width = x.shape
    group = 4 * HEAD_DIM
    n = width // group
    heads = width // HEAD_DIM
    col = lambda rows: pl.BlockSpec((rows, group), lambda g: (0, g))
    low = jax.ShapeDtypeStruct((tokens, width), BF16)
    return pl.pallas_call(
        attn_kernel,
        out_shape=(
            low, low, low,
            jax.ShapeDtypeStruct((heads, tokens, tokens), BF16),
            jax.ShapeDtypeStruct((tokens, width), F32),
            low,
            jax.ShapeDtypeStruct((tokens, width), F32),
            jax.ShapeDtypeStruct((tokens, 1), F32),
        ),
        grid=(n,),
        in_specs=[
            whole((tokens, width)), whole((tokens, 2 * HEAD_DIM)),
            col(width), col(1), col(width), col(width), col(1),
            pl.BlockSpec((group, width), lambda g: (g, 0)), whole((1, width)),
        ],
        out_specs=[
            col(tokens), col(tokens), col(tokens),
            pl.BlockSpec((4, tokens, tokens), lambda g: (g, 0, 0)),
            col(tokens), col(tokens), whole((tokens, width)), whole((tokens, 1)),
        ],
        scratch_shapes=[pltpu.VMEM((tokens, width), F32)],
        compiler_params=pltpu.CompilerParams(vmem_limit_bytes=14 << 20),
        name="attention_forward",
    )(x, bias, wq, bq, wk, wv, bv, wo, bo)


def down_kernel(ROWS, slots, gpre, slope, hat, gain1, shift1, wo, gi, ibias, keep, send, gb_s, nt_s):
    f = pl.program_id(0)
    tokens, width = hat.shape

    @pl.when(f == 0)
    def _():
        gb_s[...] = gpre[...].astype(BF16)
        nt_s[...] = (hat[...] * gain1[...] + shift1[...]).astype(BF16).T

    sums = jnp.zeros((8, width), F32)
    for r in range(0, tokens, ROWS):
        rows = slice(r, r + ROWS)
        low = (dot(gb_s[rows], wo[...], (1, 1)) * slope[rows].astype(F32)).astype(BF16)
        gi[rows] = low
        sums = sums + fold8(low.astype(F32))
    ibias[...] = jnp.sum(sums, 0, keepdims=True)
    put_units(keep, send, slots, 0, dot(nt_s[...], gi[...]), f)


def ffn_down(n_dp, slots, gpre, slope, hat, gain1, shift1, wo, ROWS=512):
    tokens, width = hat.shape
    ff = wo.shape[0]
    nf = ff // width
    vector = whole((1, width))
    full = whole((tokens, width))
    piece = pl.BlockSpec((tokens, width), lambda f, s: (0, f))
    shape = (n_dp, nf, width // (2 * n_dp), width)
    units = jax.ShapeDtypeStruct(shape, BF16)
    return pl.pallas_call(
        lambda *refs: down_kernel(ROWS, *refs),
        out_shape=(
            jax.ShapeDtypeStruct((tokens, ff), BF16),
            jax.ShapeDtypeStruct((1, ff), F32),
            units, units,
        ),
        grid_spec=pltpu.PrefetchScalarGridSpec(
            num_scalar_prefetch=1,
            grid=(nf,),
            in_specs=[
                full, piece, full, vector, vector,
                pl.BlockSpec((width, width), lambda f, s: (f, 0)),
            ],
            out_specs=[
                piece,
                pl.BlockSpec((1, width), lambda f, s: (0, f)),
                whole(shape), whole(shape),
            ],
            scratch_shapes=[
                pltpu.VMEM((tokens, width), BF16),
                pltpu.VMEM((width, tokens), BF16),
            ],
        ),
        compiler_params=pltpu.CompilerParams(vmem_limit_bytes=8 << 20),
        name="ffn_down",
    )(slots, gpre, slope, hat, gain1, shift1, wo)


def mid_kernel(slots, gpre, gi, hat, r1, gain1, wi, wa, ctx, gmid, gctx, vec, keep, send, acc_s, gb_s):
    f = pl.program_id(0)
    tokens, width = hat.shape
    more = dot(gi[...], wi[...], (1, 1))

    @pl.when(f == 0)
    def _():
        acc_s[...] = gpre[...] + more

    @pl.when(f > 0)
    def _():
        acc_s[...] += more

    @pl.when(f == pl.num_programs(0) - 1)
    def _():
        step = LN_ROWS

        def body(i, sums):
            rows = pl.ds(pl.multiple_of(i * step, step), step)
            n = hat[rows]
            g = acc_s[rows]
            gz = norm_back(g * gain1[...], n, r1[rows])
            gmid[rows] = gz
            low = gz.astype(BF16)
            gb_s[rows] = low
            return sums[0] + fold8(low.astype(F32)), sums[1] + fold8(g * n), sums[2] + fold8(g)

        zero = jnp.zeros((8, width), F32)
        sums = lax.fori_loop(0, tokens // step, body, (zero, zero, zero))
        for k in range(3):
            vec[k : k + 1] = jnp.sum(sums[k], 0, keepdims=True)
        gctx[...] = dot(gb_s[...], wa[...], (1, 1)).astype(BF16)
        put_units(keep, send, slots, 0, dot(ctx[...].T, gb_s[...]), 0)


def middle(n_dp, slots, gpre, gi, hat, r1, gain1, wi, wa, ctx):
    tokens, width = hat.shape
    nf = wi.shape[1] // width
    full = whole((tokens, width))
    shape = (n_dp, 1, width // (2 * n_dp), width)
    units = jax.ShapeDtypeStruct(shape, BF16)
    return pl.pallas_call(
        mid_kernel,
        out_shape=(
            jax.ShapeDtypeStruct((tokens, width), F32),
            jax.ShapeDtypeStruct((tokens, width), BF16),
            jax.ShapeDtypeStruct((8, width), F32),
            units, units,
        ),
        grid_spec=pltpu.PrefetchScalarGridSpec(
            num_scalar_prefetch=1,
            grid=(nf,),
            in_specs=[
                full,
                pl.BlockSpec((tokens, width), lambda f, s: (0, f)),
                full, whole((tokens, 1)), whole((1, width)),
                pl.BlockSpec((width, width), lambda f, s: (0, f)),
                whole((width, width)), full,
            ],
            out_specs=[full, full, whole((8, width)), whole(shape), whole(shape)],
            scratch_shapes=[pltpu.VMEM((tokens, width), F32), pltpu.VMEM((tokens, width), BF16)],
        ),
        compiler_params=pltpu.CompilerParams(vmem_limit_bytes=12 << 20),
        name="middle",
    )(slots, gpre, gi, hat, r1, gain1, wi, wa, ctx)


def back_kernel(slots, x, q, k, v, c, gc, inv, e, dq, dk, dv, qb, vb, keep, send, xt_s):
    g = pl.program_id(0)
    scale = 1.0 / math.sqrt(HEAD_DIM)
    pair_width = 2 * HEAD_DIM

    @pl.when(g == 0)
    def _():
        xt_s[...] = x[...].T

    low = lax.broadcasted_iota(jnp.int32, (1, pair_width), 1) < HEAD_DIM
    mine = (low, jnp.logical_not(low))
    nil = jnp.zeros((), BF16)
    for pair in range(q.shape[1] // pair_width):
        cols = slice(pair * pair_width, (pair + 1) * pair_width)
        q2, k2, v2 = q[:, cols], k[:, cols], v[:, cols]
        scaled = gc[:, cols].astype(F32) * inv[:, cols]
        prod = scaled * c[:, cols].astype(F32)
        g2 = scaled.astype(BF16)
        qt, gt = q2.T, g2.T
        dkt, dvt, total = [], [], None
        for h in range(2):
            rows = slice(h * HEAD_DIM, (h + 1) * HEAD_DIM)
            eh = e[pair * 2 + h]
            delta = jnp.sum(jnp.where(mine[h], prod, 0.0), -1, keepdims=True)
            dp = dot(jnp.where(mine[h], g2, nil), v2, (1, 1))
            ds = (eh.astype(F32) * (dp - delta)).astype(BF16)
            part = dot(ds, jnp.where(mine[h], k2, nil))
            total = part if total is None else total + part
            dvt.append(dot(gt[rows], eh))
            dkt.append(dot(qt[rows], ds))
        dq[:, cols] = (total * scale).astype(BF16)
        dv[:, cols] = jnp.concatenate(dvt, 0).astype(BF16).T
        dk[:, cols] = jnp.concatenate(dkt, 0).astype(BF16).T
    qb[...] = jnp.sum(fold8(dq[...].astype(F32)), 0, keepdims=True)
    vb[...] = jnp.sum(fold8(dv[...].astype(F32)), 0, keepdims=True)
    width = q.shape[1]
    cols = pl.ds(pl.multiple_of(g * width, width), width)
    for n, grad in enumerate((dq, dk, dv)):
        put_units(keep, send, slots, 0, dot(xt_s[...], grad[...]), n, cols)


def attention_back(n_dp, slots, x, q, k, v, c, gc, inv, e):
    tokens, width = x.shape
    group = 4 * HEAD_DIM
    col = pl.BlockSpec((tokens, group), lambda g, s: (0, g))
    row = pl.BlockSpec((1, group), lambda g, s: (0, g))
    low = jax.ShapeDtypeStruct((tokens, width), BF16)
    vector = jax.ShapeDtypeStruct((1, width), F32)
    shape = (n_dp, 3, width // (2 * n_dp), width)
    units = jax.ShapeDtypeStruct(shape, BF16)
    return pl.pallas_call(
        back_kernel,
        out_shape=(low, low, low, vector, vector, units, units),
        grid_spec=pltpu.PrefetchScalarGridSpec(
            num_scalar_prefetch=1,
            grid=(width // group,),
            in_specs=[whole((tokens, width)), col, col, col, col, col, col,
                      pl.BlockSpec((4, tokens, tokens), lambda g, s: (g, 0, 0))],
            out_specs=[col, col, col, row, row, whole(shape), whole(shape)],
            scratch_shapes=[pltpu.VMEM((width, tokens), BF16)],
        ),
        compiler_params=pltpu.CompilerParams(vmem_limit_bytes=12 << 20),
        name="attention_back",
    )(slots, x, q, k, v, c, gc, inv, e)


def input_kernel(gmid, dq, dk, dv, wq, wk, wv, out):
    total = gmid[...] + dot(dq[...], wq[...], (1, 1))
    total = total + dot(dk[...], wk[...], (1, 1))
    out[...] = (total + dot(dv[...], wv[...], (1, 1))).astype(BF16)


def input_gradient(gmid, dq, dk, dv, wq, wk, wv):
    tokens, width = gmid.shape
    group = 256
    act = whole((tokens, width))
    col = pl.BlockSpec((tokens, group), lambda i: (0, i))
    weight = pl.BlockSpec((group, width), lambda i: (i, 0))
    return pl.pallas_call(
        input_kernel,
        out_shape=jax.ShapeDtypeStruct((tokens, width), BF16),
        grid=(width // group,),
        in_specs=[col, act, act, act, weight, weight, weight],
        out_specs=col,
        compiler_params=pltpu.CompilerParams(vmem_limit_bytes=4 << 20),
        name="input_gradient",
    )(gmid, dq, dk, dv, wq, wk, wv)


def pairs(n_dp, n_seq, partner):
    out = []
    for d in range(n_dp):
        for s in range(n_seq):
            e, t = partner(d, s)
            out.append((d * n_seq + s, e * n_seq + t))
    return out


def pick(blocks, index):
    return lax.dynamic_index_in_dim(blocks, index, 0, keepdims=False)


def after(values, *others):
    return lax.optimization_barrier((values, others))[0]


def exchange(blocks, n_seq):
    return [blocks[0]] + [
        lax.ppermute(blocks[k], "seq", [(s, s ^ k) for s in range(n_seq)]) for k in range(1, n_seq)
    ]


def bit_orders(n_dp):
    bits = list(range(n_dp.bit_length() - 1))
    return bits, bits[1::-1] + bits[2:]


def slot_table(n_dp, d, s):
    orders = bit_orders(n_dp)
    odd = (s & 1) == 1
    by_core = []
    for order in orders:
        entries = []
        for j in range(n_dp):
            slot = 0
            for bit in order:
                slot = slot * 2 + (((d ^ j) >> bit) & 1)
            entries.append(slot)
        by_core.append(jnp.stack(entries))
    kept = jnp.where(odd, by_core[1], by_core[0])
    sent = jnp.where(odd, by_core[0], by_core[1])
    return jnp.concatenate([(s & 1)[None], kept, sent]).astype(jnp.int32)


def added(pieces, cut):
    total = pieces[0][cut].astype(F32)
    for piece in pieces[1:]:
        total = total + piece[cut].astype(F32)
    return total.astype(BF16)


class Halving:
    def __init__(self, keep, send, n_dp, n_seq):
        self.n_dp = n_dp
        self.n_seq = n_seq
        self.flips = [
            lambda d, s, zero=zero, one=one: (d ^ (1 << (one if s & 1 else zero)), s)
            for zero, one in zip(*bit_orders(n_dp))
        ]
        self.families = [[keep, self.permute(send, lambda d, s: (d, s ^ 1))]]

    def permute(self, values, partner):
        return lax.ppermute(values, BOTH, pairs(self.n_dp, self.n_seq, partner))

    def join(self, other):
        self.families += other.families

    def sums(self, cut):
        return jnp.concatenate([added(pieces, cut) for pieces in self.families], 1)

    def step(self, *wait):
        half = self.families[0][0].shape[0] // 2
        send = self.sums(slice(half, None))
        got = self.permute(after(send, *wait) if wait else send, self.flips.pop(0))
        families, first = [], 0
        for pieces in self.families:
            n = pieces[0].shape[1]
            families.append([piece[:half] for piece in pieces] + [got[:, first : first + n]])
            first += n
        self.families = families
        return got

    def share_y(self):
        mine = self.sums(slice(None))[0]
        got = self.permute(mine, lambda d, s: (d, s ^ 2))
        self.mine = (mine.astype(F32) + got.astype(F32)).astype(BF16)
        return got

    def share_core(self):
        other = self.permute(self.mine, lambda d, s: (d, s ^ 1))
        odd = (lax.axis_index("seq") & 1) == 1
        first = jnp.where(odd, other, self.mine)
        second = jnp.where(odd, self.mine, other)
        return jnp.concatenate([first, second], 1).astype(F32)


def sum_all(values, n_dp, n_seq):
    flips = [lambda d, s, k=k: (d, s ^ k) for k in (1, 2)]
    for bit in range(n_dp.bit_length() - 1):
        flips.append(lambda d, s, bit=bit: (d ^ (1 << bit), s))
    for flip in flips:
        values = values + lax.ppermute(values, BOTH, pairs(n_dp, n_seq, flip))
    return values


def local(
    hidden_states,
    lengths,
    query_weight,
    query_bias,
    key_weight,
    value_weight,
    value_bias,
    out_weight,
    out_bias,
    attn_gain,
    attn_shift,
    inner_weight,
    inner_bias,
    outer_weight,
    outer_bias,
    ffn_gain,
    ffn_shift,
    cotangent,
):
    _, slice_rows, width = hidden_states.shape
    n_seq = lax.axis_size("seq")
    n_dp = lax.axis_size("dp")
    d = lax.axis_index("dp")
    s = lax.axis_index("seq")
    tokens = slice_rows * n_seq
    slots = slot_table(n_dp, d, s)

    def to_passage(values):
        blocks = exchange([pick(values, s ^ k) for k in range(n_seq)], n_seq)
        return jnp.concatenate(blocks, 0)

    def to_slots(values):
        values = values.reshape(n_seq, slice_rows, width)
        blocks = exchange([values[k] for k in range(n_seq)], n_seq)
        odd = (s & 1) == 1
        high = (s & 2) == 2
        low = [jnp.where(odd, blocks[k ^ 1], blocks[k]) for k in range(4)]
        return jnp.stack([jnp.where(high, low[k ^ 2], low[k]) for k in range(4)])

    def row(vector):
        return vector.reshape(1, -1)

    x = to_passage(hidden_states)
    cot = to_passage(after(cotangent, x))
    spots = lax.iota(jnp.int32, tokens)
    spots = ((spots // slice_rows) ^ s) * slice_rows + spots % slice_rows
    bias = jnp.where(spots < pick(lengths, s), 0.0, MASKED).astype(BF16)
    bias = jnp.broadcast_to(bias.reshape(tokens, 1), (tokens, 2 * HEAD_DIM))

    query, key, value, exps, inverse, context, hat, r1 = attention_forward(
        x, bias, query_weight, row(query_bias), key_weight, value_weight, row(value_bias),
        out_weight, row(out_bias),
    )
    gain1, shift1 = row(attn_gain), row(attn_shift)
    result, slope, grad_pre, vec2, *outer_units = ffn_up(
        n_dp, slots, hat, gain1, shift1, inner_weight, row(inner_bias), outer_weight,
        row(outer_bias), row(ffn_gain), row(ffn_shift), cot,
    )
    outer = Halving(*outer_units, n_dp, n_seq)
    grad_inner, ibias, *inner_units = ffn_down(
        n_dp, slots, grad_pre, slope, hat, gain1, shift1, outer_weight
    )
    inner = Halving(*inner_units, n_dp, n_seq)
    a1 = outer.step()
    grad_mid, grad_context, vec1, *out_units = middle(
        n_dp, slots, grad_pre, grad_inner, hat, r1, gain1, inner_weight, out_weight, context,
    )
    inner.join(Halving(*out_units, n_dp, n_seq))
    a2 = outer.step()
    b1 = inner.step()
    grad_query, grad_key, grad_value, qbias, vbias, *attn_units = attention_back(
        n_dp, slots, x, query, key, value, context, grad_context, inverse, exps,
    )
    attn = Halving(*attn_units, n_dp, n_seq)
    input_low = input_gradient(
        grad_mid, grad_query, grad_key, grad_value, query_weight, key_weight, value_weight,
    )
    vectors = jnp.concatenate([vec2[:3], vec1[:3], qbias, vbias, ibias.reshape(4, width)], 0)
    c1 = attn.step()
    b2 = inner.step()
    a3 = outer.step()
    c2 = attn.step()
    b3 = inner.step()
    outer.share_y()
    c3 = attn.step()
    while attn.flips:
        attn.step()
        inner.step()
        outer.step()
    inner.share_y()
    attn.share_y()
    vectors = sum_all(vectors, n_dp, n_seq)
    block_output = to_slots(result)
    input_grad = to_slots(input_low)
    outer_sum = outer.share_core()
    inner_sum = inner.share_core()
    attn_sum = attn.share_core()
    part = width // n_dp
    mine = lax.dynamic_slice_in_dim(vectors[:8], d * part, part, 1)
    ibias_part = lax.dynamic_slice_in_dim(vectors[8:].reshape(4 * width), d * 4 * part, 4 * part, 0)
    return (
        block_output,
        input_grad,
        attn_sum[0],
        mine[6],
        attn_sum[1],
        attn_sum[2],
        mine[7],
        inner_sum[4],
        mine[3],
        mine[4],
        mine[5],
        jnp.concatenate([inner_sum[t] for t in range(4)], 1),
        ibias_part,
        outer_sum[0],
        mine[0],
        mine[1],
        mine[2],
    )


def solution(mesh):
    tokens = P("dp", "seq", None)
    in_specs = (tokens, P("dp")) + (P(),) * 15 + (tokens,)
    rows = P("dp", None)
    vector = P("dp")
    out_specs = (
        tokens, tokens, rows, vector, rows, rows, vector, rows, vector,
        vector, vector, rows, vector, rows, vector, vector, vector,
    )
    return jax.shard_map(local, mesh=mesh, in_specs=in_specs, out_specs=out_specs, check_vma=False)
```

```python
import math

import jax
import jax.numpy as jnp
from jax import lax
from jax.experimental import pallas as pl
from jax.experimental.pallas import tpu as pltpu
from jax.sharding import PartitionSpec as P

HEAD_DIM = 64
EPSILON = 1e-12
MASKED = -1e30
BF16 = jnp.bfloat16
F32 = jnp.float32
BOTH = ("dp", "seq")


LN_ROWS = 256

TAIL = (
    0.11283793300390244, 0.11283480376005173, 0.10392128676176071, 0.08427156507968903, 0.07071308046579361,
    -0.0027973579708486795, 0.08453421294689178, -0.0914449393749237, 0.025129476562142372,
)


def dot(left, right, contract=(1, 0)):
    return lax.dot_general(
        left, right, (((contract[0],), (contract[1],)), ((), ())), preferred_element_type=F32
    )


def gelu_and_slope(x):
    t = 1.0 / (1.0 + (0.4 / math.sqrt(2.0)) * jnp.abs(x))
    bell = jnp.exp2(x * x * (-0.5 * math.log2(math.e)))
    poly = TAIL[-1]
    for c in TAIL[-2::-1]:
        poly = poly * t + c
    tail = poly * t * bell
    cdf = jnp.where(x < 0.0, tail, 1.0 - tail)
    return x * cdf, cdf + x * bell * (1.0 / math.sqrt(2.0 * math.pi))


def normalize(z):
    center = z - jnp.mean(z, -1, keepdims=True)
    r = lax.rsqrt(jnp.mean(center * center, -1, keepdims=True) + EPSILON)
    return center * r, r


def norm_back(c, n, r):
    return r * (c - jnp.mean(c, -1, keepdims=True) - n * jnp.mean(c * n, -1, keepdims=True))


def fold8(x):
    return jnp.sum(x.reshape(x.shape[0] // 8, 8, x.shape[1]), 0)


def put_units(keep, send, slots, base, full, which, cols=slice(None)):
    n_dp = keep.shape[0]
    h = keep.shape[2]
    odd = slots[0] == 1
    low = full.astype(BF16)
    for m in range(full.shape[0] // (2 * h)):
        first = low[2 * m * h : (2 * m + 1) * h]
        second = low[(2 * m + 1) * h : (2 * m + 2) * h]
        keep[slots[1 + base + m], which, :, cols] = jnp.where(odd, second, first)
        send[slots[1 + n_dp + base + m], which, :, cols] = jnp.where(odd, first, second)


def up_kernel(ROWS, slots, hat, gain1, shift1, wi, bi, wo, bo, gain2, shift2, cot,
              result, slope, gpre, vec, keep, send, act_s, low_s, acc_s, gb_s):
    f = pl.program_id(0)
    nf = act_s.shape[0]
    tokens = hat.shape[0]

    @pl.when(f == 0)
    def _():
        normed = hat[...] * gain1[...] + shift1[...]
        low_s[...] = normed.astype(BF16)
        acc_s[...] = normed + bo[...]

    @pl.when(f < nf)
    def _():
        for r in range(0, tokens, ROWS):
            rows = slice(r, r + ROWS)
            act, slow = gelu_and_slope(dot(low_s[rows], wi[...]) + bi[...])
            act = act.astype(BF16)
            act_s[f, rows] = act
            slope[rows] = slow.astype(BF16)
            acc_s[rows] += dot(act, wo[...])

    @pl.when(f == nf - 1)
    def _():
        step = LN_ROWS

        def body(i, sums):
            rows = pl.ds(pl.multiple_of(i * step, step), step)
            n, r = normalize(acc_s[rows])
            result[rows] = (n * gain2[...] + shift2[...]).astype(BF16)
            g = cot[rows].astype(F32)
            gz = norm_back(g * gain2[...], n, r)
            gpre[rows] = gz
            low = gz.astype(BF16)
            gb_s[rows] = low
            return sums[0] + fold8(low.astype(F32)), sums[1] + fold8(g * n), sums[2] + fold8(g)

        zero = jnp.zeros((8, hat.shape[1]), F32)
        sums = lax.fori_loop(0, tokens // step, body, (zero, zero, zero))
        vec[...] = jnp.zeros_like(vec)
        for k in range(3):
            vec[k : k + 1] = jnp.sum(sums[k], 0, keepdims=True)

    @pl.when(f >= nf)
    def _():
        blocks = keep.shape[0] // nf
        put_units(keep, send, slots, (f - nf) * blocks, dot(act_s[f - nf], gb_s[...], (0, 0)), 0)


def whole(shape):
    return pl.BlockSpec(shape, lambda *_: (0,) * len(shape))


def ffn_up(n_dp, slots, hat, gain1, shift1, wi, bi, wo, bo, gain2, shift2, cot, ROWS=512):
    tokens, width = hat.shape
    ff = wi.shape[1]
    nf = ff // width
    half = ff // (2 * n_dp)
    step = lambda f: jnp.minimum(f, nf - 1)
    vector = whole((1, width))
    return pl.pallas_call(
        lambda *refs: up_kernel(ROWS, *refs),
        out_shape=(
            jax.ShapeDtypeStruct((tokens, width), BF16),
            jax.ShapeDtypeStruct((tokens, ff), BF16),
            jax.ShapeDtypeStruct((tokens, width), F32),
            jax.ShapeDtypeStruct((8, width), F32),
            jax.ShapeDtypeStruct((n_dp, 1, half, width), BF16),
            jax.ShapeDtypeStruct((n_dp, 1, half, width), BF16),
        ),
        grid_spec=pltpu.PrefetchScalarGridSpec(
            num_scalar_prefetch=1,
            grid=(2 * nf,),
            in_specs=[
                whole((tokens, width)), vector, vector,
                pl.BlockSpec((width, width), lambda f, s: (0, step(f))),
                pl.BlockSpec((1, width), lambda f, s: (0, step(f))),
                pl.BlockSpec((width, width), lambda f, s: (step(f), 0)),
                vector, vector, vector, whole((tokens, width)),
            ],
            out_specs=[
                whole((tokens, width)),
                pl.BlockSpec((tokens, width), lambda f, s: (0, step(f))),
                whole((tokens, width)),
                whole((8, width)),
                whole((n_dp, 1, half, width)),
                whole((n_dp, 1, half, width)),
            ],
            scratch_shapes=[
                pltpu.VMEM((nf, tokens, width), BF16),
                pltpu.VMEM((tokens, width), BF16),
                pltpu.VMEM((tokens, width), F32),
                pltpu.VMEM((tokens, width), BF16),
            ],
        ),
        compiler_params=pltpu.CompilerParams(vmem_limit_bytes=20 << 20),
        name="ffn_up",
    )(slots, hat, gain1, shift1, wi, bi, wo, bo, gain2, shift2, cot)


def attn_kernel(x, bias, wq, bq, wk, wv, bv, wo, bo,
                q_out, k_out, v_out, e_out, inv_out, c_out, hat_out, r_out, acc_s):
    g = pl.program_id(0)
    tokens = x.shape[0]
    xs = x[...]
    qs = (dot(xs, wq[...]) + bq[...]).astype(BF16) * (1.0 / math.sqrt(HEAD_DIM))
    ks = dot(xs, wk[...]).astype(BF16)
    vs = (dot(xs, wv[...]) + bv[...]).astype(BF16)
    q_out[...] = qs
    k_out[...] = ks
    v_out[...] = vs
    lanes = lax.broadcasted_iota(jnp.int32, (1, 2 * HEAD_DIM), 1)
    low = lanes < HEAD_DIM
    mine = (low, jnp.logical_not(low))
    nil = jnp.zeros((), BF16)
    one = jnp.ones((), BF16)
    for pair in range(qs.shape[1] // (2 * HEAD_DIM)):
        cols = slice(pair * 2 * HEAD_DIM, (pair + 1) * 2 * HEAD_DIM)
        q2, k2, v2 = qs[:, cols], ks[:, cols], vs[:, cols]
        sums = []
        for h in range(2):
            spare = lanes == (HEAD_DIM if h == 0 else 0)
            qa = jnp.where(mine[h], q2, jnp.where(spare, one, nil))
            ka = jnp.where(mine[h], k2, jnp.where(spare, bias[...], nil))
            s = dot(qa, ka, (1, 1))
            e = jnp.exp(s - jnp.max(s, -1, keepdims=True)).astype(BF16)
            e_out[pair * 2 + h] = e
            sums.append(dot(e, jnp.where(mine[h], v2, one)))
        inv = 1.0 / pltpu.roll(jnp.where(low, sums[1], sums[0]), HEAD_DIM, 1)
        inv_out[:, cols] = inv
        c_out[:, cols] = (jnp.where(low, sums[0], sums[1]) * inv).astype(BF16)
    more = dot(c_out[...], wo[...])

    @pl.when(g == 0)
    def _():
        acc_s[...] = xs.astype(F32) + bo[...] + more

    @pl.when(g > 0)
    def _():
        acc_s[...] += more

    @pl.when(g == pl.num_programs(0) - 1)
    def _():
        step = LN_ROWS

        def body(i, _):
            rows = pl.ds(pl.multiple_of(i * step, step), step)
            n, r = normalize(acc_s[rows])
            hat_out[rows] = n
            r_out[rows] = r
            return 0

        lax.fori_loop(0, tokens // step, body, 0)


def attention_forward(x, bias, wq, bq, wk, wv, bv, wo, bo):
    tokens, width = x.shape
    group = 4 * HEAD_DIM
    n = width // group
    heads = width // HEAD_DIM
    col = lambda rows: pl.BlockSpec((rows, group), lambda g: (0, g))
    low = jax.ShapeDtypeStruct((tokens, width), BF16)
    far = pltpu.HBM((tokens, width), BF16)
    return pl.pallas_call(
        attn_kernel,
        out_shape=(
            far, far, far,
            pltpu.HBM((heads, tokens, tokens), BF16),
            pltpu.HBM((tokens, width), F32),
            low,
            jax.ShapeDtypeStruct((tokens, width), F32),
            jax.ShapeDtypeStruct((tokens, 1), F32),
        ),
        grid=(n,),
        in_specs=[
            whole((tokens, width)), whole((tokens, 2 * HEAD_DIM)),
            col(width), col(1), col(width), col(width), col(1),
            pl.BlockSpec((group, width), lambda g: (g, 0)), whole((1, width)),
        ],
        out_specs=[
            col(tokens), col(tokens), col(tokens),
            pl.BlockSpec((4, tokens, tokens), lambda g: (g, 0, 0)),
            col(tokens), col(tokens), whole((tokens, width)), whole((tokens, 1)),
        ],
        scratch_shapes=[pltpu.VMEM((tokens, width), F32)],
        compiler_params=pltpu.CompilerParams(vmem_limit_bytes=14 << 20),
        name="attention_forward",
    )(x, bias, wq, bq, wk, wv, bv, wo, bo)


def down_kernel(ROWS, slots, gpre, slope, hat, gain1, shift1, wo, gi, ibias, keep, send, gb_s, nt_s):
    f = pl.program_id(0)
    tokens, width = hat.shape

    @pl.when(f == 0)
    def _():
        gb_s[...] = gpre[...].astype(BF16)
        nt_s[...] = (hat[...] * gain1[...] + shift1[...]).astype(BF16).T
        ibias[...] = jnp.zeros_like(ibias)

    sums = jnp.zeros((8, width), F32)
    for r in range(0, tokens, ROWS):
        rows = slice(r, r + ROWS)
        low = (dot(gb_s[rows], wo[...], (1, 1)) * slope[rows].astype(F32)).astype(BF16)
        gi[rows] = low
        sums = sums + fold8(low.astype(F32))
    ibias[pl.ds(f, 1)] = jnp.sum(sums, 0, keepdims=True)
    put_units(keep, send, slots, 0, dot(nt_s[...], gi[...]), f ^ slots[slots.shape[0] - 1])


def ffn_down(n_dp, slots, gpre, slope, hat, gain1, shift1, wo, ROWS=512):
    tokens, width = hat.shape
    ff = wo.shape[0]
    nf = ff // width
    vector = whole((1, width))
    full = whole((tokens, width))
    piece = pl.BlockSpec((tokens, width), lambda f, s: (0, f))
    shape = (n_dp, nf, width // (2 * n_dp), width)
    units = jax.ShapeDtypeStruct(shape, BF16)
    return pl.pallas_call(
        lambda *refs: down_kernel(ROWS, *refs),
        out_shape=(
            jax.ShapeDtypeStruct((tokens, ff), BF16),
            jax.ShapeDtypeStruct((8, width), F32),
            units, units,
        ),
        grid_spec=pltpu.PrefetchScalarGridSpec(
            num_scalar_prefetch=1,
            grid=(nf,),
            in_specs=[
                full, piece, full, vector, vector,
                pl.BlockSpec((width, width), lambda f, s: (f, 0)),
            ],
            out_specs=[
                piece, whole((8, width)), whole(shape), whole(shape),
            ],
            scratch_shapes=[
                pltpu.VMEM((tokens, width), BF16),
                pltpu.VMEM((width, tokens), BF16),
            ],
        ),
        compiler_params=pltpu.CompilerParams(vmem_limit_bytes=8 << 20),
        name="ffn_down",
    )(slots, gpre, slope, hat, gain1, shift1, wo)


def mid_kernel(slots, gpre, gi, hat, r1, gain1, wi, wa, ctx, gmid, gctx, vec, keep, send, acc_s, gb_s):
    f = pl.program_id(0)
    tokens, width = hat.shape
    more = dot(gi[...], wi[...], (1, 1))

    @pl.when(f == 0)
    def _():
        acc_s[...] = gpre[...] + more

    @pl.when(f > 0)
    def _():
        acc_s[...] += more

    @pl.when(f == pl.num_programs(0) - 1)
    def _():
        step = LN_ROWS

        def body(i, sums):
            rows = pl.ds(pl.multiple_of(i * step, step), step)
            n = hat[rows]
            g = acc_s[rows]
            gz = norm_back(g * gain1[...], n, r1[rows])
            gmid[rows] = gz
            low = gz.astype(BF16)
            gb_s[rows] = low
            return sums[0] + fold8(low.astype(F32)), sums[1] + fold8(g * n), sums[2] + fold8(g)

        zero = jnp.zeros((8, width), F32)
        sums = lax.fori_loop(0, tokens // step, body, (zero, zero, zero))
        vec[...] = jnp.zeros_like(vec)
        for k in range(3):
            vec[k : k + 1] = jnp.sum(sums[k], 0, keepdims=True)
        gctx[...] = dot(gb_s[...], wa[...], (1, 1)).astype(BF16)
        put_units(keep, send, slots, 0, dot(ctx[...].T, gb_s[...]), 0)


def middle(n_dp, slots, gpre, gi, hat, r1, gain1, wi, wa, ctx):
    tokens, width = hat.shape
    nf = wi.shape[1] // width
    full = whole((tokens, width))
    shape = (n_dp, 1, width // (2 * n_dp), width)
    units = jax.ShapeDtypeStruct(shape, BF16)
    return pl.pallas_call(
        mid_kernel,
        out_shape=(
            jax.ShapeDtypeStruct((tokens, width), F32),
            jax.ShapeDtypeStruct((tokens, width), BF16),
            jax.ShapeDtypeStruct((8, width), F32),
            units, units,
        ),
        grid_spec=pltpu.PrefetchScalarGridSpec(
            num_scalar_prefetch=1,
            grid=(nf,),
            in_specs=[
                full,
                pl.BlockSpec((tokens, width), lambda f, s: (0, f)),
                full, whole((tokens, 1)), whole((1, width)),
                pl.BlockSpec((width, width), lambda f, s: (0, f)),
                whole((width, width)), full,
            ],
            out_specs=[full, full, whole((8, width)), whole(shape), whole(shape)],
            scratch_shapes=[pltpu.VMEM((tokens, width), F32), pltpu.VMEM((tokens, width), BF16)],
        ),
        compiler_params=pltpu.CompilerParams(vmem_limit_bytes=12 << 20),
        name="middle",
    )(slots, gpre, gi, hat, r1, gain1, wi, wa, ctx)


def back_kernel(q, k, v, c, gc, inv, e, dq, dk, dv, vec):
    scale = 1.0 / math.sqrt(HEAD_DIM)
    pair_width = 2 * HEAD_DIM

    low = lax.broadcasted_iota(jnp.int32, (1, pair_width), 1) < HEAD_DIM
    mine = (low, jnp.logical_not(low))
    nil = jnp.zeros((), BF16)
    for pair in range(q.shape[1] // pair_width):
        cols = slice(pair * pair_width, (pair + 1) * pair_width)
        q2, k2, v2 = q[:, cols], k[:, cols], v[:, cols]
        scaled = gc[:, cols].astype(F32) * inv[:, cols]
        prod = scaled * c[:, cols].astype(F32)
        g2 = scaled.astype(BF16)
        qt, gt = q2.T, g2.T
        dkt, dvt, total = [], [], None
        for h in range(2):
            rows = slice(h * HEAD_DIM, (h + 1) * HEAD_DIM)
            eh = e[pair * 2 + h]
            delta = jnp.sum(jnp.where(mine[h], prod, 0.0), -1, keepdims=True)
            dp = dot(jnp.where(mine[h], g2, nil), v2, (1, 1))
            ds = (eh.astype(F32) * (dp - delta)).astype(BF16)
            part = dot(ds, jnp.where(mine[h], k2, nil))
            total = part if total is None else total + part
            dvt.append(dot(gt[rows], eh))
            dkt.append(dot(qt[rows], ds))
        dq[:, cols] = (total * scale).astype(BF16)
        dv[:, cols] = jnp.concatenate(dvt, 0).astype(BF16).T
        dk[:, cols] = jnp.concatenate(dkt, 0).astype(BF16).T
    vec[...] = jnp.zeros_like(vec)
    vec[0:1] = jnp.sum(fold8(dq[...].astype(F32)), 0, keepdims=True)
    vec[1:2] = jnp.sum(fold8(dv[...].astype(F32)), 0, keepdims=True)


def attention_back(q, k, v, c, gc, inv, e):
    tokens, width = q.shape
    group = 4 * HEAD_DIM
    col = pl.BlockSpec((tokens, group), lambda g: (0, g))
    low = jax.ShapeDtypeStruct((tokens, width), BF16)
    return pl.pallas_call(
        back_kernel,
        out_shape=(low, low, low, jax.ShapeDtypeStruct((8, width), F32)),
        grid=(width // group,),
        in_specs=[col, col, col, col, col, col,
                  pl.BlockSpec((4, tokens, tokens), lambda g: (g, 0, 0))],
        out_specs=[col, col, col, pl.BlockSpec((8, group), lambda g: (0, g))],
        compiler_params=pltpu.CompilerParams(vmem_limit_bytes=12 << 20),
        name="attention_back",
    )(q, k, v, c, gc, inv, e)


def weights_kernel(slots, x, dq, dk, dv, vec2, vec1, ibias, vec0, keep, send, vkeep, vsend):
    xt = x[...].T
    for n, grad in enumerate((dq, dk, dv)):
        put_units(keep, send, slots, 0, dot(xt, grad[...]), n)
    n_dp = keep.shape[0]
    width = x.shape[1]
    part = width // n_dp
    odd = slots[0] == 1
    eight = jnp.concatenate([vec2[0:3], vec1[0:3], vec0[0:2]], 0)

    def two(rows):
        high = rows.astype(BF16).astype(F32)
        return jnp.concatenate([high, rows - high], 0).astype(BF16)

    for j in range(n_dp):
        start = 4 * part * j
        row = ibias[start // width : start // width + 1]
        row = jnp.broadcast_to(row, (8, width))
        first = two(pltpu.roll(eight, (width - part * j) % width, 1))
        second = two(pltpu.roll(row, (width - start % width) % width, 1))
        vkeep[slots[1 + j]] = jnp.where(odd, second, first)
        vsend[slots[1 + n_dp + j]] = jnp.where(odd, first, second)


def weight_gradients(n_dp, slots, x, dq, dk, dv, *vectors):
    tokens, width = x.shape
    full = whole((tokens, width))
    shape = (n_dp, 3, width // (2 * n_dp), width)
    tiny = (n_dp, 16, width)
    units = jax.ShapeDtypeStruct(shape, BF16)
    small = jax.ShapeDtypeStruct(tiny, BF16)
    return pl.pallas_call(
        weights_kernel,
        out_shape=(units, units, small, small),
        grid_spec=pltpu.PrefetchScalarGridSpec(
            num_scalar_prefetch=1,
            grid=(1,),
            in_specs=[full, full, full, full] + [whole((8, width))] * 4,
            out_specs=[whole(shape), whole(shape), whole(tiny), whole(tiny)],
        ),
        compiler_params=pltpu.CompilerParams(vmem_limit_bytes=12 << 20),
        name="weight_gradients",
    )(slots, x, dq, dk, dv, *vectors)


def input_kernel(gmid, dq, dk, dv, wq, wk, wv, out):
    total = gmid[...] + dot(dq[...], wq[...], (1, 1))
    total = total + dot(dk[...], wk[...], (1, 1))
    out[...] = (total + dot(dv[...], wv[...], (1, 1))).astype(BF16)


def input_gradient(gmid, dq, dk, dv, wq, wk, wv):
    tokens, width = gmid.shape
    group = 256
    act = whole((tokens, width))
    col = pl.BlockSpec((tokens, group), lambda i: (0, i))
    weight = pl.BlockSpec((group, width), lambda i: (i, 0))
    return pl.pallas_call(
        input_kernel,
        out_shape=jax.ShapeDtypeStruct((tokens, width), BF16),
        grid=(width // group,),
        in_specs=[col, act, act, act, weight, weight, weight],
        out_specs=col,
        compiler_params=pltpu.CompilerParams(vmem_limit_bytes=4 << 20),
        name="input_gradient",
    )(gmid, dq, dk, dv, wq, wk, wv)


def pairs(n_dp, n_seq, partner):
    out = []
    for d in range(n_dp):
        for s in range(n_seq):
            e, t = partner(d, s)
            out.append((d * n_seq + s, e * n_seq + t))
    return out


def pick(blocks, index):
    return lax.dynamic_index_in_dim(blocks, index, 0, keepdims=False)


def after(values, *others):
    return lax.optimization_barrier((values, others))[0]


def exchange(blocks, n_seq):
    return [blocks[0]] + [
        lax.ppermute(blocks[k], "seq", [(s, s ^ k) for s in range(n_seq)]) for k in range(1, n_seq)
    ]


def bit_orders(n_dp):
    bits = list(range(n_dp.bit_length() - 1))
    return bits, bits[1::-1] + bits[2:]


def slot_table(n_dp, d, s):
    orders = bit_orders(n_dp)
    odd = (s & 1) == 1
    by_core = []
    for order in orders:
        entries = []
        for j in range(n_dp):
            slot = 0
            for bit in order:
                slot = slot * 2 + (((d ^ j) >> bit) & 1)
            entries.append(slot)
        by_core.append(jnp.stack(entries))
    kept = jnp.where(odd, by_core[1], by_core[0])
    sent = jnp.where(odd, by_core[0], by_core[1])
    return jnp.concatenate([(s & 1)[None], kept, sent, (s & 2)[None]]).astype(jnp.int32)


def added(pieces, cut):
    total = pieces[0][cut].astype(F32)
    for piece in pieces[1:]:
        total = total + piece[cut].astype(F32)
    return total.astype(BF16)


def added_in_two(pieces, cut):
    total = 0.0
    for piece in pieces:
        rows = piece[cut].astype(F32)
        total = total + (rows[..., :8, :] + rows[..., 8:, :])
    high = total.astype(BF16)
    return jnp.concatenate([high, (total - high.astype(F32)).astype(BF16)], -2)


class Halving:
    def __init__(self, keep, send, n_dp, n_seq, small=()):
        self.y_cut = False
        self.n_dp = n_dp
        self.n_seq = n_seq
        self.flips = [
            lambda d, s, zero=zero, one=one: (d ^ (1 << (one if s & 1 else zero)), s)
            for zero, one in zip(*bit_orders(n_dp))
        ]
        flat = lambda units: units.reshape(n_dp, -1, units.shape[-1])
        keep, send = flat(keep), flat(send)
        rows = keep.shape[1]
        self.adders = [added]
        self.families = [[keep]]
        if small:
            self.adders.append(added_in_two)
            self.families.append([small[0]])
            send = jnp.concatenate([send, small[1]], 1)
        self.take(self.permute(send, lambda d, s: (d, s ^ 1)))

    def permute(self, values, partner):
        return lax.ppermute(values, BOTH, pairs(self.n_dp, self.n_seq, partner))

    def take(self, got):
        for pieces, part in zip(self.families, self.split(got)):
            pieces.append(part)

    def join(self, other):
        self.families += other.families
        self.adders += other.adders

    def sums(self, cut):
        parts = [add(pieces, cut) for add, pieces in zip(self.adders, self.families)]
        return parts[0] if len(parts) == 1 else jnp.concatenate(parts, -2)

    def cut_y(self):
        half = self.families[0][0].shape[1] // 2
        self.y_cut = True
        got = self.permute(
            self.sums((slice(None), slice(half, None))), lambda d, s: (d, s ^ 2)
        )
        self.families[0] = [piece[:, :half] for piece in self.families[0]]
        self.take(got)

    def step(self):
        half = self.families[0][0].shape[0] // 2
        got = self.permute(self.sums(slice(half, None)), self.flips.pop(0))
        self.families = [[piece[:half] for piece in pieces] for pieces in self.families]
        self.take(got)

    def share_y(self):
        mine = self.sums(0)
        got = self.permute(mine, lambda d, s: (d, s ^ 2))
        self.families = [[piece] for piece in self.split(mine)]
        self.take(got)
        if not self.y_cut:
            self.mine = self.sums(Ellipsis)
            return
        high = (lax.axis_index("seq") & 2) == 2
        own, other = self.families[0]
        both = [jnp.where(high, other, own), jnp.where(high, own, other)]
        rest = [add(p, Ellipsis) for add, p in zip(self.adders[1:], self.families[1:])]
        self.mine = jnp.concatenate(both + rest, -2)
        self.families[0] = [jnp.concatenate(both, -2)]

    def split(self, values):
        parts, first = [], 0
        for pieces in self.families:
            rows = pieces[0].shape[-2]
            parts.append(values[..., first : first + rows, :])
            first += rows
        return parts

    def share_core(self):
        other = self.permute(self.mine, lambda d, s: (d, s ^ 1))
        odd = (lax.axis_index("seq") & 1) == 1
        halves = (jnp.where(odd, other, self.mine), jnp.where(odd, self.mine, other))
        return [[part.astype(F32) for part in pair] for pair in zip(*map(self.split, halves))]


def joined(pair, count):
    first, second = (half.reshape(count, -1, half.shape[-1]) for half in pair)
    return jnp.concatenate([first, second], 1)


def local(
    hidden_states,
    lengths,
    query_weight,
    query_bias,
    key_weight,
    value_weight,
    value_bias,
    out_weight,
    out_bias,
    attn_gain,
    attn_shift,
    inner_weight,
    inner_bias,
    outer_weight,
    outer_bias,
    ffn_gain,
    ffn_shift,
    cotangent,
):
    _, slice_rows, width = hidden_states.shape
    n_seq = lax.axis_size("seq")
    n_dp = lax.axis_size("dp")
    d = lax.axis_index("dp")
    s = lax.axis_index("seq")
    tokens = slice_rows * n_seq
    slots = slot_table(n_dp, d, s)

    def to_passage(values, *wait):
        blocks = [pick(values, s ^ k) for k in range(n_seq)]
        return jnp.concatenate(exchange(after(blocks, *wait), n_seq), 0)

    def to_slots(values):
        values = values.reshape(n_seq, slice_rows, width)
        blocks = exchange([values[k] for k in range(n_seq)], n_seq)
        odd = (s & 1) == 1
        high = (s & 2) == 2
        low = [jnp.where(odd, blocks[k ^ 1], blocks[k]) for k in range(4)]
        return jnp.stack([jnp.where(high, low[k ^ 2], low[k]) for k in range(4)])

    def row(vector):
        return vector.reshape(1, -1)

    x = to_passage(hidden_states)
    cot = to_passage(cotangent, x)
    spots = lax.iota(jnp.int32, tokens)
    spots = ((spots // slice_rows) ^ s) * slice_rows + spots % slice_rows
    bias = jnp.where(spots < pick(lengths, s), 0.0, MASKED).astype(BF16)
    bias = jnp.broadcast_to(bias.reshape(tokens, 1), (tokens, 2 * HEAD_DIM))

    query, key, value, exps, inverse, context, hat, r1 = attention_forward(
        x, bias, query_weight, row(query_bias), key_weight, value_weight, row(value_bias),
        out_weight, row(out_bias),
    )
    gain1, shift1 = row(attn_gain), row(attn_shift)
    result, slope, grad_pre, vec2, *outer_units = ffn_up(
        n_dp, slots, hat, gain1, shift1, inner_weight, row(inner_bias), outer_weight,
        row(outer_bias), row(ffn_gain), row(ffn_shift), cot,
    )
    outer = Halving(*outer_units, n_dp, n_seq)
    grad_inner, ibias, *inner_units = ffn_down(
        n_dp, slots, grad_pre, slope, hat, gain1, shift1, outer_weight
    )
    inner = Halving(*inner_units, n_dp, n_seq)
    a1 = outer.step()
    grad_mid, grad_context, vec1, *out_units = middle(
        n_dp, slots, grad_pre, grad_inner, hat, r1, gain1, inner_weight, out_weight, context,
    )
    inner.cut_y()
    inner.join(Halving(*out_units, n_dp, n_seq))
    grad_query, grad_key, grad_value, vec0 = attention_back(
        query, key, value, context, grad_context, inverse, exps,
    )
    outer.step()
    keep, send, *small = weight_gradients(
        n_dp, slots, x, grad_query, grad_key, grad_value, vec2, vec1, ibias, vec0,
    )
    attn = Halving(keep, send, n_dp, n_seq, small)
    input_low = input_gradient(
        grad_mid, grad_query, grad_key, grad_value, query_weight, key_weight, value_weight,
    )
    for group in (attn, inner, outer):
        while group.flips:
            group.step()
        group.share_y()
    block_output = to_slots(result)
    input_grad = to_slots(input_low)
    ((outer_pair),) = outer.share_core()
    inner_pair, out_pair = inner.share_core()
    attn_pair, small_pair = attn.share_core()
    outer_sum = joined(outer_pair, 1)[0]
    inner_sum = joined(inner_pair, 4)
    attn_sum = joined(attn_pair, 3)
    part = width // n_dp
    small_sum = [half[:8] + half[8:] for half in small_pair]
    mine = small_sum[0][:, :part]
    return (
        block_output,
        input_grad,
        attn_sum[0],
        mine[6],
        attn_sum[1],
        attn_sum[2],
        mine[7],
        joined(out_pair, 1)[0],
        mine[3],
        mine[4],
        mine[5],
        jnp.concatenate([inner_sum[t] for t in range(4)], 1),
        small_sum[1][0, : 4 * part],
        outer_sum,
        mine[0],
        mine[1],
        mine[2],
    )


def solution(mesh):
    tokens = P("dp", "seq", None)
    in_specs = (tokens, P("dp")) + (P(),) * 15 + (tokens,)
    rows = P("dp", None)
    vector = P("dp")
    out_specs = (
        tokens, tokens, rows, vector, rows, rows, vector, rows, vector,
        vector, vector, rows, vector, rows, vector, vector, vector,
    )
    return jax.shard_map(local, mesh=mesh, in_specs=in_specs, out_specs=out_specs, check_vma=False)
```

```python
import math

import jax
import jax.numpy as jnp
from jax import lax
from jax.experimental import pallas as pl
from jax.experimental.pallas import tpu as pltpu
from jax.sharding import PartitionSpec as P

HEAD_DIM = 64
EPSILON = 1e-12
MASKED = -1e30
BF16 = jnp.bfloat16
F32 = jnp.float32
BOTH = ("dp", "seq")


LN_ROWS = 256

TAIL = (
    0.11283793300390244, 0.11283480376005173, 0.10392128676176071, 0.08427156507968903, 0.07071308046579361,
    -0.0027973579708486795, 0.08453421294689178, -0.0914449393749237, 0.025129476562142372,
)


def dot(left, right, contract=(1, 0)):
    return lax.dot_general(
        left, right, (((contract[0],), (contract[1],)), ((), ())), preferred_element_type=F32
    )


def gelu_and_slope(x):
    t = 1.0 / (1.0 + (0.4 / math.sqrt(2.0)) * jnp.abs(x))
    bell = jnp.exp2(x * x * (-0.5 * math.log2(math.e)))
    poly = TAIL[-1]
    for c in TAIL[-2::-1]:
        poly = poly * t + c
    tail = poly * t * bell
    cdf = jnp.where(x < 0.0, tail, 1.0 - tail)
    return x * cdf, cdf + x * bell * (1.0 / math.sqrt(2.0 * math.pi))


def normalize(z):
    center = z - jnp.mean(z, -1, keepdims=True)
    r = lax.rsqrt(jnp.mean(center * center, -1, keepdims=True) + EPSILON)
    return center * r, r


def norm_back(c, n, r):
    return r * (c - jnp.mean(c, -1, keepdims=True) - n * jnp.mean(c * n, -1, keepdims=True))


def fold8(x):
    return jnp.sum(x.reshape(x.shape[0] // 8, 8, x.shape[1]), 0)


def put_units(keep, send, slots, base, full, which, cols=slice(None)):
    n_dp = keep.shape[0]
    h = keep.shape[2]
    odd = slots[0] == 1
    low = full.astype(BF16)
    for m in range(full.shape[0] // (2 * h)):
        first = low[2 * m * h : (2 * m + 1) * h]
        second = low[(2 * m + 1) * h : (2 * m + 2) * h]
        keep[slots[1 + base + m], which, :, cols] = jnp.where(odd, second, first)
        send[slots[1 + n_dp + base + m], which, :, cols] = jnp.where(odd, first, second)


def up_kernel(ROWS, slots, hat, gain1, shift1, wi, bi, wo, bo, gain2, shift2, cot,
              result, slope, gpre, vec, keep, send, act_s, low_s, acc_s, gb_s):
    f = pl.program_id(0)
    nf = act_s.shape[0]
    tokens = hat.shape[0]

    @pl.when(f == 0)
    def _():
        normed = hat[...] * gain1[...] + shift1[...]
        low_s[...] = normed.astype(BF16)
        acc_s[...] = normed + bo[...]

    @pl.when(f < nf)
    def _():
        for r in range(0, tokens, ROWS):
            rows = slice(r, r + ROWS)
            act, slow = gelu_and_slope(dot(low_s[rows], wi[...]) + bi[...])
            act = act.astype(BF16)
            act_s[f, rows] = act
            slope[rows] = slow.astype(BF16)
            acc_s[rows] += dot(act, wo[...])

    @pl.when(f == nf - 1)
    def _():
        step = LN_ROWS

        def body(i, sums):
            rows = pl.ds(pl.multiple_of(i * step, step), step)
            n, r = normalize(acc_s[rows])
            result[rows] = (n * gain2[...] + shift2[...]).astype(BF16)
            g = cot[rows].astype(F32)
            gz = norm_back(g * gain2[...], n, r)
            gpre[rows] = gz
            low = gz.astype(BF16)
            gb_s[rows] = low
            return sums[0] + fold8(low.astype(F32)), sums[1] + fold8(g * n), sums[2] + fold8(g)

        zero = jnp.zeros((8, hat.shape[1]), F32)
        sums = lax.fori_loop(0, tokens // step, body, (zero, zero, zero))
        vec[...] = jnp.zeros_like(vec)
        for k in range(3):
            vec[k : k + 1] = jnp.sum(sums[k], 0, keepdims=True)

    @pl.when(f >= nf)
    def _():
        blocks = keep.shape[0] // nf
        put_units(keep, send, slots, (f - nf) * blocks, dot(act_s[f - nf], gb_s[...], (0, 0)), 0)


def whole(shape):
    return pl.BlockSpec(shape, lambda *_: (0,) * len(shape))


def ffn_up(n_dp, slots, hat, gain1, shift1, wi, bi, wo, bo, gain2, shift2, cot, ROWS=512):
    tokens, width = hat.shape
    ff = wi.shape[1]
    nf = ff // width
    half = ff // (2 * n_dp)
    step = lambda f: jnp.minimum(f, nf - 1)
    vector = whole((1, width))
    return pl.pallas_call(
        lambda *refs: up_kernel(ROWS, *refs),
        out_shape=(
            jax.ShapeDtypeStruct((tokens, width), BF16),
            jax.ShapeDtypeStruct((tokens, ff), BF16),
            jax.ShapeDtypeStruct((tokens, width), F32),
            jax.ShapeDtypeStruct((8, width), F32),
            jax.ShapeDtypeStruct((n_dp, 1, half, width), BF16),
            jax.ShapeDtypeStruct((n_dp, 1, half, width), BF16),
        ),
        grid_spec=pltpu.PrefetchScalarGridSpec(
            num_scalar_prefetch=1,
            grid=(2 * nf,),
            in_specs=[
                whole((tokens, width)), vector, vector,
                pl.BlockSpec((width, width), lambda f, s: (0, step(f))),
                pl.BlockSpec((1, width), lambda f, s: (0, step(f))),
                pl.BlockSpec((width, width), lambda f, s: (step(f), 0)),
                vector, vector, vector, whole((tokens, width)),
            ],
            out_specs=[
                whole((tokens, width)),
                pl.BlockSpec((tokens, width), lambda f, s: (0, step(f))),
                whole((tokens, width)),
                whole((8, width)),
                whole((n_dp, 1, half, width)),
                whole((n_dp, 1, half, width)),
            ],
            scratch_shapes=[
                pltpu.VMEM((nf, tokens, width), BF16),
                pltpu.VMEM((tokens, width), BF16),
                pltpu.VMEM((tokens, width), F32),
                pltpu.VMEM((tokens, width), BF16),
            ],
        ),
        compiler_params=pltpu.CompilerParams(vmem_limit_bytes=20 << 20),
        name="ffn_up",
    )(slots, hat, gain1, shift1, wi, bi, wo, bo, gain2, shift2, cot)


def attn_kernel(x, bias, wq, bq, wk, wv, bv, wo, bo,
                q_out, k_out, v_out, e_out, inv_out, c_out, hat_out, r_out, acc_s):
    g = pl.program_id(0)
    tokens = x.shape[0]
    xs = x[...]
    qs = (dot(xs, wq[...]) + bq[...]).astype(BF16) * (1.0 / math.sqrt(HEAD_DIM))
    ks = dot(xs, wk[...]).astype(BF16)
    vs = (dot(xs, wv[...]) + bv[...]).astype(BF16)
    q_out[...] = qs
    k_out[...] = ks
    v_out[...] = vs
    lanes = lax.broadcasted_iota(jnp.int32, (1, 2 * HEAD_DIM), 1)
    low = lanes < HEAD_DIM
    mine = (low, jnp.logical_not(low))
    nil = jnp.zeros((), BF16)
    one = jnp.ones((), BF16)
    for pair in range(qs.shape[1] // (2 * HEAD_DIM)):
        cols = slice(pair * 2 * HEAD_DIM, (pair + 1) * 2 * HEAD_DIM)
        q2, k2, v2 = qs[:, cols], ks[:, cols], vs[:, cols]
        sums = []
        for h in range(2):
            spare = lanes == (HEAD_DIM if h == 0 else 0)
            qa = jnp.where(mine[h], q2, jnp.where(spare, one, nil))
            ka = jnp.where(mine[h], k2, jnp.where(spare, bias[...], nil))
            s = dot(qa, ka, (1, 1))
            e = jnp.exp(s - jnp.max(s, -1, keepdims=True)).astype(BF16)
            e_out[pair * 2 + h] = e
            sums.append(dot(e, jnp.where(mine[h], v2, one)))
        inv = 1.0 / pltpu.roll(jnp.where(low, sums[1], sums[0]), HEAD_DIM, 1)
        inv_out[:, cols] = inv
        c_out[:, cols] = (jnp.where(low, sums[0], sums[1]) * inv).astype(BF16)
    more = dot(c_out[...], wo[...])

    @pl.when(g == 0)
    def _():
        acc_s[...] = xs.astype(F32) + bo[...] + more

    @pl.when(g > 0)
    def _():
        acc_s[...] += more

    @pl.when(g == pl.num_programs(0) - 1)
    def _():
        step = LN_ROWS

        def body(i, _):
            rows = pl.ds(pl.multiple_of(i * step, step), step)
            n, r = normalize(acc_s[rows])
            hat_out[rows] = n
            r_out[rows] = r
            return 0

        lax.fori_loop(0, tokens // step, body, 0)


def attention_forward(x, bias, wq, bq, wk, wv, bv, wo, bo):
    tokens, width = x.shape
    group = 4 * HEAD_DIM
    n = width // group
    heads = width // HEAD_DIM
    col = lambda rows: pl.BlockSpec((rows, group), lambda g: (0, g))
    low = jax.ShapeDtypeStruct((tokens, width), BF16)
    far = pltpu.HBM((tokens, width), BF16)
    wq, wk, wv = (pltpu.with_memory_space_constraint(w, pltpu.HBM) for w in (wq, wk, wv))
    return pl.pallas_call(
        attn_kernel,
        out_shape=(
            far, far, far,
            pltpu.HBM((heads, tokens, tokens), BF16),
            pltpu.HBM((tokens, width), F32),
            low,
            jax.ShapeDtypeStruct((tokens, width), F32),
            jax.ShapeDtypeStruct((tokens, 1), F32),
        ),
        grid=(n,),
        in_specs=[
            whole((tokens, width)), whole((tokens, 2 * HEAD_DIM)),
            col(width), col(1), col(width), col(width), col(1),
            pl.BlockSpec((group, width), lambda g: (g, 0)), whole((1, width)),
        ],
        out_specs=[
            col(tokens), col(tokens), col(tokens),
            pl.BlockSpec((4, tokens, tokens), lambda g: (g, 0, 0)),
            col(tokens), col(tokens), whole((tokens, width)), whole((tokens, 1)),
        ],
        scratch_shapes=[pltpu.VMEM((tokens, width), F32)],
        compiler_params=pltpu.CompilerParams(vmem_limit_bytes=17 << 20),
        name="attention_forward",
    )(x, bias, wq, bq, wk, wv, bv, wo, bo)


def down_kernel(ROWS, slots, gpre, slope, hat, gain1, shift1, wo, gi, ibias, keep, send, gb_s, nt_s):
    f = pl.program_id(0)
    tokens, width = hat.shape

    @pl.when(f == 0)
    def _():
        gb_s[...] = gpre[...].astype(BF16)
        nt_s[...] = (hat[...] * gain1[...] + shift1[...]).astype(BF16).T
        ibias[...] = jnp.zeros_like(ibias)

    sums = jnp.zeros((8, width), F32)
    for r in range(0, tokens, ROWS):
        rows = slice(r, r + ROWS)
        low = (dot(gb_s[rows], wo[...], (1, 1)) * slope[rows].astype(F32)).astype(BF16)
        gi[rows] = low
        sums = sums + fold8(low.astype(F32))
    ibias[pl.ds(f, 1)] = jnp.sum(sums, 0, keepdims=True)
    put_units(keep, send, slots, 0, dot(nt_s[...], gi[...]), f ^ slots[slots.shape[0] - 1])


def ffn_down(n_dp, slots, gpre, slope, hat, gain1, shift1, wo, ROWS=512):
    tokens, width = hat.shape
    ff = wo.shape[0]
    nf = ff // width
    vector = whole((1, width))
    full = whole((tokens, width))
    piece = pl.BlockSpec((tokens, width), lambda f, s: (0, f))
    shape = (n_dp, nf, width // (2 * n_dp), width)
    units = jax.ShapeDtypeStruct(shape, BF16)
    return pl.pallas_call(
        lambda *refs: down_kernel(ROWS, *refs),
        out_shape=(
            jax.ShapeDtypeStruct((tokens, ff), BF16),
            jax.ShapeDtypeStruct((8, width), F32),
            units, units,
        ),
        grid_spec=pltpu.PrefetchScalarGridSpec(
            num_scalar_prefetch=1,
            grid=(nf,),
            in_specs=[
                full, piece, full, vector, vector,
                pl.BlockSpec((width, width), lambda f, s: (f, 0)),
            ],
            out_specs=[
                piece, whole((8, width)), whole(shape), whole(shape),
            ],
            scratch_shapes=[
                pltpu.VMEM((tokens, width), BF16),
                pltpu.VMEM((width, tokens), BF16),
            ],
        ),
        compiler_params=pltpu.CompilerParams(vmem_limit_bytes=8 << 20),
        name="ffn_down",
    )(slots, gpre, slope, hat, gain1, shift1, wo)


def mid_kernel(slots, gpre, gi, hat, r1, gain1, wi, wa, ctx, gmid, gctx, vec, keep, send, acc_s, gb_s):
    f = pl.program_id(0)
    tokens, width = hat.shape
    more = dot(gi[...], wi[...], (1, 1))

    @pl.when(f == 0)
    def _():
        acc_s[...] = gpre[...] + more

    @pl.when(f > 0)
    def _():
        acc_s[...] += more

    @pl.when(f == pl.num_programs(0) - 1)
    def _():
        step = LN_ROWS

        def body(i, sums):
            rows = pl.ds(pl.multiple_of(i * step, step), step)
            n = hat[rows]
            g = acc_s[rows]
            gz = norm_back(g * gain1[...], n, r1[rows])
            gmid[rows] = gz
            low = gz.astype(BF16)
            gb_s[rows] = low
            return sums[0] + fold8(low.astype(F32)), sums[1] + fold8(g * n), sums[2] + fold8(g)

        zero = jnp.zeros((8, width), F32)
        sums = lax.fori_loop(0, tokens // step, body, (zero, zero, zero))
        vec[...] = jnp.zeros_like(vec)
        for k in range(3):
            vec[k : k + 1] = jnp.sum(sums[k], 0, keepdims=True)
        gctx[...] = dot(gb_s[...], wa[...], (1, 1)).astype(BF16)
        put_units(keep, send, slots, 0, dot(ctx[...].T, gb_s[...]), 0)


def middle(n_dp, slots, gpre, gi, hat, r1, gain1, wi, wa, ctx):
    tokens, width = hat.shape
    nf = wi.shape[1] // width
    full = whole((tokens, width))
    shape = (n_dp, 1, width // (2 * n_dp), width)
    units = jax.ShapeDtypeStruct(shape, BF16)
    return pl.pallas_call(
        mid_kernel,
        out_shape=(
            jax.ShapeDtypeStruct((tokens, width), F32),
            jax.ShapeDtypeStruct((tokens, width), BF16),
            jax.ShapeDtypeStruct((8, width), F32),
            units, units,
        ),
        grid_spec=pltpu.PrefetchScalarGridSpec(
            num_scalar_prefetch=1,
            grid=(nf,),
            in_specs=[
                full,
                pl.BlockSpec((tokens, width), lambda f, s: (0, f)),
                full, whole((tokens, 1)), whole((1, width)),
                pl.BlockSpec((width, width), lambda f, s: (0, f)),
                whole((width, width)), full,
            ],
            out_specs=[full, full, whole((8, width)), whole(shape), whole(shape)],
            scratch_shapes=[pltpu.VMEM((tokens, width), F32), pltpu.VMEM((tokens, width), BF16)],
        ),
        compiler_params=pltpu.CompilerParams(vmem_limit_bytes=12 << 20),
        name="middle",
    )(slots, gpre, gi, hat, r1, gain1, wi, wa, ctx)


def back_kernel(q, k, v, c, gc, inv, e, dq, dk, dv, vec):
    scale = 1.0 / math.sqrt(HEAD_DIM)
    pair_width = 2 * HEAD_DIM

    low = lax.broadcasted_iota(jnp.int32, (1, pair_width), 1) < HEAD_DIM
    mine = (low, jnp.logical_not(low))
    nil = jnp.zeros((), BF16)
    for pair in range(q.shape[1] // pair_width):
        cols = slice(pair * pair_width, (pair + 1) * pair_width)
        q2, k2, v2 = q[:, cols], k[:, cols], v[:, cols]
        scaled = gc[:, cols].astype(F32) * inv[:, cols]
        prod = scaled * c[:, cols].astype(F32)
        g2 = scaled.astype(BF16)
        qt, gt = q2.T, g2.T
        dkt, dvt, total = [], [], None
        for h in range(2):
            rows = slice(h * HEAD_DIM, (h + 1) * HEAD_DIM)
            eh = e[pair * 2 + h]
            delta = jnp.sum(jnp.where(mine[h], prod, 0.0), -1, keepdims=True)
            dp = dot(jnp.where(mine[h], g2, nil), v2, (1, 1))
            ds = (eh.astype(F32) * (dp - delta)).astype(BF16)
            part = dot(ds, jnp.where(mine[h], k2, nil))
            total = part if total is None else total + part
            dvt.append(dot(gt[rows], eh))
            dkt.append(dot(qt[rows], ds))
        dq[:, cols] = (total * scale).astype(BF16)
        dv[:, cols] = jnp.concatenate(dvt, 0).astype(BF16).T
        dk[:, cols] = jnp.concatenate(dkt, 0).astype(BF16).T
    vec[...] = jnp.zeros_like(vec)
    vec[0:1] = jnp.sum(fold8(dq[...].astype(F32)), 0, keepdims=True)
    vec[1:2] = jnp.sum(fold8(dv[...].astype(F32)), 0, keepdims=True)


def attention_back(q, k, v, c, gc, inv, e):
    tokens, width = q.shape
    group = 4 * HEAD_DIM
    col = pl.BlockSpec((tokens, group), lambda g: (0, g))
    low = jax.ShapeDtypeStruct((tokens, width), BF16)
    return pl.pallas_call(
        back_kernel,
        out_shape=(low, low, low, jax.ShapeDtypeStruct((8, width), F32)),
        grid=(width // group,),
        in_specs=[col, col, col, col, col, col,
                  pl.BlockSpec((4, tokens, tokens), lambda g: (g, 0, 0))],
        out_specs=[col, col, col, pl.BlockSpec((8, group), lambda g: (0, g))],
        compiler_params=pltpu.CompilerParams(vmem_limit_bytes=12 << 20),
        name="attention_back",
    )(q, k, v, c, gc, inv, e)


def weights_kernel(slots, x, dq, dk, dv, vec2, vec1, ibias, vec0, keep, send):
    n_dp = keep.shape[0]
    width = x.shape[1]
    h = width // (2 * n_dp)
    odd = slots[0] == 1
    xt = x[...].T
    for n, grad in enumerate((dq, dk, dv)):
        low = dot(xt, grad[...]).astype(BF16)
        rows = slice(n * h, (n + 1) * h)
        for j in range(n_dp):
            first = low[2 * j * h : (2 * j + 1) * h]
            second = low[(2 * j + 1) * h : (2 * j + 2) * h]
            keep[slots[1 + j], rows] = jnp.where(odd, second, first)
            send[slots[1 + n_dp + j], rows] = jnp.where(odd, first, second)
    part = width // n_dp
    eight = jnp.concatenate([vec2[0:3], vec1[0:3], vec0[0:2]], 0)

    def two(rows):
        high = rows.astype(BF16).astype(F32)
        return jnp.concatenate([high, rows - high], 0).astype(BF16)

    for j in range(n_dp):
        start = 4 * part * j
        row = ibias[start // width : start // width + 1]
        row = jnp.broadcast_to(row, (8, width))
        first = two(pltpu.roll(eight, (width - part * j) % width, 1))
        second = two(pltpu.roll(row, (width - start % width) % width, 1))
        keep[slots[1 + j], 3 * h :] = jnp.where(odd, second, first)
        send[slots[1 + n_dp + j], 3 * h :] = jnp.where(odd, first, second)


def weight_gradients(n_dp, slots, x, dq, dk, dv, *vectors):
    tokens, width = x.shape
    full = whole((tokens, width))
    shape = (n_dp, 3 * (width // (2 * n_dp)) + 16, width)
    units = jax.ShapeDtypeStruct(shape, BF16)
    return pl.pallas_call(
        weights_kernel,
        out_shape=(units, units),
        grid_spec=pltpu.PrefetchScalarGridSpec(
            num_scalar_prefetch=1,
            grid=(1,),
            in_specs=[full, full, full, full] + [whole((8, width))] * 4,
            out_specs=[whole(shape), whole(shape)],
        ),
        compiler_params=pltpu.CompilerParams(vmem_limit_bytes=12 << 20),
        name="weight_gradients",
    )(slots, x, dq, dk, dv, *vectors)


def input_kernel(gmid, dq, dk, dv, wq, wk, wv, out):
    total = gmid[...] + dot(dq[...], wq[...], (1, 1))
    total = total + dot(dk[...], wk[...], (1, 1))
    out[...] = (total + dot(dv[...], wv[...], (1, 1))).astype(BF16)


def input_gradient(gmid, dq, dk, dv, wq, wk, wv):
    tokens, width = gmid.shape
    group = 256
    act = whole((tokens, width))
    col = pl.BlockSpec((tokens, group), lambda i: (0, i))
    weight = pl.BlockSpec((group, width), lambda i: (i, 0))
    return pl.pallas_call(
        input_kernel,
        out_shape=jax.ShapeDtypeStruct((tokens, width), BF16),
        grid=(width // group,),
        in_specs=[col, act, act, act, weight, weight, weight],
        out_specs=col,
        compiler_params=pltpu.CompilerParams(vmem_limit_bytes=4 << 20),
        name="input_gradient",
    )(gmid, dq, dk, dv, wq, wk, wv)


def pairs(n_dp, n_seq, partner):
    out = []
    for d in range(n_dp):
        for s in range(n_seq):
            e, t = partner(d, s)
            out.append((d * n_seq + s, e * n_seq + t))
    return out


def pick(blocks, index):
    return lax.dynamic_index_in_dim(blocks, index, 0, keepdims=False)


def after(values, *others):
    return lax.optimization_barrier((values, others))[0]


def exchange(blocks, n_seq):
    return [blocks[0]] + [
        lax.ppermute(blocks[k], "seq", [(s, s ^ k) for s in range(n_seq)]) for k in range(1, n_seq)
    ]


def bit_orders(n_dp):
    bits = list(range(n_dp.bit_length() - 1))
    return bits, bits[1::-1] + bits[2:]


def slot_table(n_dp, d, s):
    orders = bit_orders(n_dp)
    odd = (s & 1) == 1
    by_core = []
    for order in orders:
        entries = []
        for j in range(n_dp):
            slot = 0
            for bit in order:
                slot = slot * 2 + (((d ^ j) >> bit) & 1)
            entries.append(slot)
        by_core.append(jnp.stack(entries))
    kept = jnp.where(odd, by_core[1], by_core[0])
    sent = jnp.where(odd, by_core[0], by_core[1])
    return jnp.concatenate([(s & 1)[None], kept, sent, (s & 2)[None]]).astype(jnp.int32)


def added(pieces, cut):
    total = pieces[0][cut].astype(F32)
    for piece in pieces[1:]:
        total = total + piece[cut].astype(F32)
    return total.astype(BF16)


def added_in_two(pieces, cut):
    total = 0.0
    for piece in pieces:
        rows = piece[cut].astype(F32)
        total = total + (rows[..., :8, :] + rows[..., 8:, :])
    high = lax.reduce_precision(total, 8, 7)
    return jnp.concatenate([high, total - high], -2).astype(BF16)


class Halving:
    def __init__(self, keep, send, n_dp, n_seq, small=0):
        self.y_cut = False
        self.n_dp = n_dp
        self.n_seq = n_seq
        self.flips = [
            lambda d, s, zero=zero, one=one: (d ^ (1 << (one if s & 1 else zero)), s)
            for zero, one in zip(*bit_orders(n_dp))
        ]
        flat = lambda units: units.reshape(n_dp, -1, units.shape[-1])
        keep, send = flat(keep), flat(send)
        self.adders = [added]
        self.families = [[keep]]
        if small:
            self.adders.append(added_in_two)
            self.families = [[keep[:, :-small]], [keep[:, -small:]]]
        self.take(self.permute(send, lambda d, s: (d, s ^ 1)))

    def permute(self, values, partner):
        return lax.ppermute(values, BOTH, pairs(self.n_dp, self.n_seq, partner))

    def take(self, got):
        for pieces, part in zip(self.families, self.split(got)):
            pieces.append(part)

    def join(self, other):
        self.families += other.families
        self.adders += other.adders

    def sums(self, cut):
        parts = [add(pieces, cut) for add, pieces in zip(self.adders, self.families)]
        return parts[0] if len(parts) == 1 else jnp.concatenate(parts, -2)

    def cut_y(self):
        half = self.families[0][0].shape[1] // 2
        self.y_cut = True
        got = self.permute(
            self.sums((slice(None), slice(half, None))), lambda d, s: (d, s ^ 2)
        )
        self.families[0] = [piece[:, :half] for piece in self.families[0]]
        self.take(got)

    def step(self):
        half = self.families[0][0].shape[0] // 2
        got = self.permute(self.sums(slice(half, None)), self.flips.pop(0))
        self.families = [[piece[:half] for piece in pieces] for pieces in self.families]
        self.take(got)

    def share_y(self):
        mine = self.sums(0)
        got = self.permute(mine, lambda d, s: (d, s ^ 2))
        self.families = [[piece] for piece in self.split(mine)]
        self.take(got)
        if not self.y_cut:
            self.mine = self.sums(Ellipsis)
            return
        high = (lax.axis_index("seq") & 2) == 2
        own, other = self.families[0]
        both = [jnp.where(high, other, own), jnp.where(high, own, other)]
        rest = [add(p, Ellipsis) for add, p in zip(self.adders[1:], self.families[1:])]
        self.mine = jnp.concatenate(both + rest, -2)
        self.families[0] = [jnp.concatenate(both, -2)]

    def split(self, values):
        parts, first = [], 0
        for pieces in self.families:
            rows = pieces[0].shape[-2]
            parts.append(values[..., first : first + rows, :])
            first += rows
        return parts

    def share_core(self):
        other = self.permute(self.mine, lambda d, s: (d, s ^ 1))
        odd = (lax.axis_index("seq") & 1) == 1
        halves = (jnp.where(odd, other, self.mine), jnp.where(odd, self.mine, other))
        return [[part.astype(F32) for part in pair] for pair in zip(*map(self.split, halves))]


def joined(pair, count):
    first, second = (half.reshape(count, -1, half.shape[-1]) for half in pair)
    return jnp.concatenate([first, second], 1)


def local(
    hidden_states,
    lengths,
    query_weight,
    query_bias,
    key_weight,
    value_weight,
    value_bias,
    out_weight,
    out_bias,
    attn_gain,
    attn_shift,
    inner_weight,
    inner_bias,
    outer_weight,
    outer_bias,
    ffn_gain,
    ffn_shift,
    cotangent,
):
    _, slice_rows, width = hidden_states.shape
    n_seq = lax.axis_size("seq")
    n_dp = lax.axis_size("dp")
    d = lax.axis_index("dp")
    s = lax.axis_index("seq")
    tokens = slice_rows * n_seq
    slots = slot_table(n_dp, d, s)

    def to_passage(values, *wait):
        blocks = [pick(values, s ^ k) for k in range(n_seq)]
        return jnp.concatenate(exchange(after(blocks, *wait), n_seq), 0)

    def to_slots(values):
        values = values.reshape(n_seq, slice_rows, width)
        blocks = exchange([values[k] for k in range(n_seq)], n_seq)
        odd = (s & 1) == 1
        high = (s & 2) == 2
        low = [jnp.where(odd, blocks[k ^ 1], blocks[k]) for k in range(4)]
        return jnp.stack([jnp.where(high, low[k ^ 2], low[k]) for k in range(4)])

    def row(vector):
        return vector.reshape(1, -1)

    x = to_passage(hidden_states)
    cot = to_passage(cotangent, x)
    spots = lax.iota(jnp.int32, tokens)
    spots = ((spots // slice_rows) ^ s) * slice_rows + spots % slice_rows
    bias = jnp.where(spots < pick(lengths, s), 0.0, MASKED).astype(BF16)
    bias = jnp.broadcast_to(bias.reshape(tokens, 1), (tokens, 2 * HEAD_DIM))

    query, key, value, exps, inverse, context, hat, r1 = attention_forward(
        x, bias, query_weight, row(query_bias), key_weight, value_weight, row(value_bias),
        out_weight, row(out_bias),
    )
    gain1, shift1 = row(attn_gain), row(attn_shift)
    result, slope, grad_pre, vec2, *outer_units = ffn_up(
        n_dp, slots, hat, gain1, shift1, inner_weight, row(inner_bias), outer_weight,
        row(outer_bias), row(ffn_gain), row(ffn_shift), cot,
    )
    outer = Halving(*outer_units, n_dp, n_seq)
    grad_inner, ibias, *inner_units = ffn_down(
        n_dp, slots, grad_pre, slope, hat, gain1, shift1, outer_weight
    )
    inner = Halving(*inner_units, n_dp, n_seq)
    a1 = outer.step()
    grad_mid, grad_context, vec1, *out_units = middle(
        n_dp, slots, grad_pre, grad_inner, hat, r1, gain1, inner_weight, out_weight, context,
    )
    inner.cut_y()
    inner.join(Halving(*out_units, n_dp, n_seq))
    grad_query, grad_key, grad_value, vec0 = attention_back(
        query, key, value, context, grad_context, inverse, exps,
    )
    outer.step()
    attn_units = weight_gradients(
        n_dp, slots, x, grad_query, grad_key, grad_value, vec2, vec1, ibias, vec0,
    )
    attn = Halving(*attn_units, n_dp, n_seq, small=16)
    input_low = input_gradient(
        grad_mid, grad_query, grad_key, grad_value, query_weight, key_weight, value_weight,
    )
    for group in (attn, inner, outer):
        while group.flips:
            group.step()
        group.share_y()
    block_output = to_slots(result)
    input_grad = to_slots(input_low)
    ((outer_pair),) = outer.share_core()
    inner_pair, out_pair = inner.share_core()
    attn_pair, small_pair = attn.share_core()
    outer_sum = joined(outer_pair, 1)[0]
    inner_sum = joined(inner_pair, 4)
    attn_sum = joined(attn_pair, 3)
    part = width // n_dp
    small_sum = [half[:8] + half[8:] for half in small_pair]
    mine = small_sum[0][:, :part]
    return (
        block_output,
        input_grad,
        attn_sum[0],
        mine[6],
        attn_sum[1],
        attn_sum[2],
        mine[7],
        joined(out_pair, 1)[0],
        mine[3],
        mine[4],
        mine[5],
        jnp.concatenate([inner_sum[t] for t in range(4)], 1),
        small_sum[1][0, : 4 * part],
        outer_sum,
        mine[0],
        mine[1],
        mine[2],
    )


def solution(mesh):
    tokens = P("dp", "seq", None)
    in_specs = (tokens, P("dp")) + (P(),) * 15 + (tokens,)
    rows = P("dp", None)
    vector = P("dp")
    out_specs = (
        tokens, tokens, rows, vector, rows, rows, vector, rows, vector,
        vector, vector, rows, vector, rows, vector, vector, vector,
    )
    return jax.shard_map(local, mesh=mesh, in_specs=in_specs, out_specs=out_specs, check_vma=False)
```
